32 devices in a mesh: groups: 2 (over y), tmpl: 4 (over z), region: 2 (over x), sub: 2 (over core).
Axes of the slice: x: 2, y: 2, z: 4, core: 2. Of those that a mesh axis runs over, the one named last changes fastest.
Arguments:
- waveforms: float32 [2, 16, 4096], P('region', ('tmpl', 'sub'), 'groups'), parts along dimension 2
- templates: bfloat16 [2, 192, 12, 400], P('region', ('tmpl', 'sub'))
- channel_ids: int32 [2, 192, 12], P('region', ('tmpl', 'sub')), may hold values from 0 to 31, as said below
- moveouts: int32 [2, 192, 12], P('region', ('tmpl', 'sub')), may hold values from 0 to 511
- active: int32 [2, 192], P('region', ('tmpl', 'sub')), may hold values from 6 to 12
- border: int32 [2, 2, 8], P('region'), may hold values from 0 to 15, as said below
- border_count: int32 [2, 2], P('region'), may hold values from 1 to 8
Outputs:
- scores: float32 [2, 192, 1024], P('region', ('tmpl', 'sub'), 'groups'), parts along dimension 2
The draws below stay inside these ranges and needn't reach their ends.
There are 2 independent parts, one for each index of `groups`. The reference program is written for one: setup_inputs(seed, part) draws one part's arguments, and reference() takes and returns one part's arrays. A program takes and returns all parts, laid end to end along the dimension named above; an argument that names none is the same for every part. Nothing has to cross between parts.
Inputs may be any that keep to these rules, and one draw needn't show every extreme that they name: `channel_ids`: the 12 entries of a template are distinct. An entry below 16 is one of the region's own channels; 16 + i is entry i of the previous region's side 1 border list and 24 + i entry i of the next region's side 0 border list; such an entry appears only where that region exists and i is below that list's border_count. `border`: each list names 8 distinct channels of its region.
All inputs are finite; a program needn't handle non-finite values.
Results may differ from the reference program's by a relative error of at most 0.0081.
Values sent between devices are 32-bit elements; how exact they have to be, the bound alone decides.
A program may use at most 64 MiB of HBM per device.

```python
import math
import jax
import jax.numpy as jnp
from jax import lax

NF = 2048
F0 = 40
BAND = 384
K = 400
SLOTS = 12
MINACT = 6
OUT = 512
SHMAX = 512
LN = 1024
REGIONS = 2
CH_REG = 16
BMAX = 8
CH_EXT = 32
TPL_REG = 192


def draw_waveforms(key, part):
    keys = jax.random.split(jax.random.fold_in(key, 11), 9)
    amplitude = jnp.exp(jax.random.uniform(keys[0], (REGIONS, CH_REG, 1), jnp.float32, 0.0, math.log(10.0)))
    centers = jax.random.uniform(keys[1], (REGIONS, CH_REG, 3, 1), jnp.float32, 0.0, NF * 1.0)
    heights = jnp.exp(jax.random.uniform(keys[2], (REGIONS, CH_REG, 3, 1), jnp.float32, 0.0, math.log(8.0)))
    samples = jnp.arange(NF, dtype=jnp.float32)[None, None, None, :]
    spread = NF / 16.0
    envelope = 1.0 + jnp.sum(heights * jnp.exp(-0.5 * jnp.square((samples - centers) / spread)), axis=2)
    noise = jax.random.normal(keys[3], (REGIONS, CH_REG, NF), jnp.float32)
    spike_on = (jax.random.randint(keys[5], (REGIONS, CH_REG, 1), 0, 100, jnp.int32) < 12).astype(jnp.float32)
    positions = jax.random.randint(keys[6], (REGIONS, CH_REG, 3, 1), 0, NF, jnp.int32)
    signs = (2 * jax.random.randint(keys[7], (REGIONS, CH_REG, 3, 1), 0, 2, jnp.int32) - 1).astype(jnp.float32)
    spike_sizes = signs * jax.random.uniform(keys[8], (REGIONS, CH_REG, 3, 1), jnp.float32, 40.0, 100.0)
    sample_ids = jnp.arange(NF, dtype=jnp.int32)[None, None, None, :]
    spikes = jnp.sum(jnp.where(sample_ids == positions, spike_sizes, 0.0), axis=2) * spike_on
    return (amplitude * (envelope * noise + spikes)).astype(jnp.float32)


def draw_templates(key, part):
    keys = jax.random.split(jax.random.fold_in(key, 22), 2)
    scaling = jnp.exp(jax.random.uniform(keys[0], (REGIONS, TPL_REG, SLOTS, 1), jnp.float32, 0.0, math.log(10.0)))
    shapes = jax.random.normal(keys[1], (REGIONS, TPL_REG, SLOTS, K), jnp.float32)
    return (scaling * shapes).astype(jnp.bfloat16)


def border_sizes(key):
    keys = jax.random.split(jax.random.fold_in(key, 33), 2)
    sizes = jax.random.randint(keys[0], (REGIONS, 2), 1, BMAX + 1, jnp.int32)
    forced = jax.random.randint(keys[1], (), 1, REGIONS, jnp.int32)
    sizes = sizes.at[forced, 0].set(BMAX)
    sizes = sizes.at[0, 0].set(1)
    return (sizes, forced)


def draw_border_count(key, part):
    return border_sizes(key)[0]


def draw_border(key, part):
    slot_ids = jnp.arange(CH_REG, dtype=jnp.int32)
    scores = jax.random.randint(jax.random.fold_in(key, 44), (REGIONS, 2, CH_REG), 0, 1 << 20, jnp.int32) * CH_REG + slot_ids
    scores = scores.at[0, 0, 0].set(1 << 30)
    scores = scores.at[0, 0, CH_REG - 1].set((1 << 30) + 1)
    return lax.top_k(scores, BMAX)[1].astype(jnp.int32)


def draw_channel_ids(key, part):
    sizes, forced = border_sizes(key)
    keys = jax.random.split(jax.random.fold_in(key, 55), 2)
    slot_ids = jnp.arange(CH_EXT, dtype=jnp.int32)[None, :]
    region_ids = jnp.arange(REGIONS, dtype=jnp.int32)[:, None]
    left_live = jnp.where(region_ids > 0, sizes[jnp.maximum(region_ids - 1, 0), 1], 0)
    right_live = jnp.where(region_ids < REGIONS - 1, sizes[jnp.minimum(region_ids + 1, REGIONS - 1), 0], 0)
    left_slot = slot_ids - CH_REG
    right_slot = slot_ids - CH_REG - BMAX
    valid = (slot_ids < CH_REG) | (left_slot >= 0) & (left_slot < BMAX) & (left_slot < left_live) | (right_slot >= 0) & (right_slot < right_live)
    scores = jax.random.randint(keys[0], (REGIONS, TPL_REG, CH_EXT), 0, 1 << 20, jnp.int32) * CH_EXT + slot_ids[None]
    scores = jnp.where(valid[:, None, :], scores, -1)
    picked = jax.random.randint(keys[1], (), 0, TPL_REG, jnp.int32)
    template_ids = jnp.arange(TPL_REG, dtype=jnp.int32)[None, :, None]
    boost = (region_ids[:, :, None] == forced - 1) & (template_ids == picked) & ((slot_ids[None] == 0) | (slot_ids[None] == CH_EXT - 1))
    scores = jnp.where(boost, (1 << 30) + slot_ids[None], scores)
    return lax.top_k(scores, SLOTS)[1].astype(jnp.int32)


def touch_ends(result, own_key, smallest, top_value):
    longest = result.shape.index(max(result.shape))
    spots = []
    for shift in (0, 1):
        where = [jax.random.randint(jax.random.fold_in(own_key, axis), (), 0, length) for axis, length in enumerate(result.shape)]
        where[longest] = (where[longest] + shift) % result.shape[longest]
        spots.append(tuple(where))
    return result.at[spots[0]].set(smallest).at[spots[1]].set(top_value)


def setup_inputs(seed: int = 0, part: int = 0) -> dict:
    seeds = jax.random.split(jax.random.key(seed), 8)
    part_splits = jax.random.split(jax.random.fold_in(seeds[7], part), 8)
    return {
        "waveforms": draw_waveforms(jax.random.fold_in(jax.random.fold_in(seeds[7], part), 71), part),
        "templates": draw_templates(jax.random.fold_in(seeds[7], 71), part),
        "channel_ids": draw_channel_ids(jax.random.fold_in(seeds[7], 71), part),
        "moveouts": touch_ends(jax.random.randint(seeds[3], (REGIONS, TPL_REG, SLOTS), 0, SHMAX), jax.random.fold_in(seeds[3], 1), 0, SHMAX - 1).astype(jnp.int32),
        "active": touch_ends(jax.random.randint(seeds[4], (REGIONS, TPL_REG), MINACT, SLOTS + 1), jax.random.fold_in(seeds[4], 1), MINACT, SLOTS).astype(jnp.int32),
        "border": draw_border(jax.random.fold_in(seeds[7], 71), part),
        "border_count": draw_border_count(jax.random.fold_in(seeds[7], 71), part),
    }


EPSILON = 1e-06

def angles(samples, first_bin, bins, length):
    sample_ids = jnp.arange(samples, dtype=jnp.int32)[:, None]
    bin_ids = first_bin + jnp.arange(bins, dtype=jnp.int32)[None, :]
    turn_count = sample_ids * bin_ids % length
    return turn_count.astype(jnp.float32) * (2.0 * math.pi / length)

def forward_table(samples, first_bin, bins, length):
    phases = angles(samples, first_bin, bins, length)
    return jnp.concatenate([jnp.cos(phases), -jnp.sin(phases)], axis=1)

def inverse_table(samples, first_bin, bins, length):
    phases = jnp.transpose(angles(samples, first_bin, bins, length))
    return jnp.concatenate([jnp.cos(phases), -jnp.sin(phases)], axis=0)

def window_energy(spectra):
    lag_rows = inverse_table(NF, F0, BAND, NF)
    filtered = 2.0 / NF * jnp.dot(spectra, lag_rows, precision=lax.Precision.HIGHEST, preferred_element_type=jnp.float32)
    running = jnp.cumsum(filtered * filtered, axis=1)
    running = jnp.concatenate([jnp.zeros((running.shape[0], 1), jnp.float32), running], axis=1)
    return running[:, K:K + LN] - running[:, :LN]

def pick_rows(payload, indices, live_count, offset):
    chosen = jnp.take(payload, indices, axis=0)
    places = offset + jnp.arange(indices.shape[0], dtype=jnp.int32)
    return jnp.where((places < live_count)[:, None], chosen, jnp.zeros_like(chosen))

def cross_spectrum(tmpl_spectra, data_spectra):
    half_bins = tmpl_spectra.shape[1] // 2
    tmpl_real = tmpl_spectra[:, :half_bins]
    tmpl_imag = tmpl_spectra[:, half_bins:]
    data_real = data_spectra[:, :half_bins]
    data_imag = data_spectra[:, half_bins:]
    return jnp.concatenate([tmpl_real * data_real + tmpl_imag * data_imag, tmpl_real * data_imag - tmpl_imag * data_real], axis=1)

def block_scores(block_items, ext_spectra, station_norm, short_table, lag_table):
    block_waves, block_ids, block_moves, block_active = block_items
    templ_count = block_waves.shape[0]
    slot_count = block_waves.shape[1]
    flat_waves = block_waves.reshape(templ_count * slot_count, block_waves.shape[2]).astype(jnp.float32)
    tmpl_spectra = jnp.dot(flat_waves, short_table, precision=lax.Precision.HIGHEST, preferred_element_type=jnp.float32)
    tmpl_norm = jnp.sqrt(lax.optimization_barrier(jnp.sum(jnp.square(flat_waves), axis=1)) + EPSILON)
    flat_ids = block_ids.reshape(-1)
    cross_terms = cross_spectrum(tmpl_spectra, jnp.take(ext_spectra, flat_ids, axis=0)).astype(jnp.bfloat16)
    cross_terms = lax.optimization_barrier(cross_terms).astype(jnp.float32)
    correlation = 2.0 / NF * jnp.dot(cross_terms, lag_table, precision=lax.Precision.HIGHEST, preferred_element_type=jnp.float32)
    normed = correlation / (tmpl_norm[:, None] * jnp.take(station_norm, flat_ids, axis=0))
    aligned = jax.vmap(lambda series, offset: lax.dynamic_slice_in_dim(series, offset, OUT))(normed, block_moves.reshape(-1).astype(jnp.int32))
    weights = (jnp.arange(slot_count, dtype=jnp.int32)[None, :] < block_active[:, None]).astype(jnp.float32)
    return lax.optimization_barrier(jnp.sum(aligned.reshape(templ_count, slot_count, OUT) * weights[:, :, None], axis=1))

def reference(waveforms, templates, channel_ids, moveouts, active, border, border_count):
    data_table = forward_table(NF, F0, BAND, NF)
    spectra = lax.map(lambda trace: jnp.dot(trace, data_table, precision=lax.Precision.HIGHEST, preferred_element_type=jnp.float32), waveforms)
    energy = lax.map(window_energy, spectra)
    payload = jnp.concatenate([spectra, energy], axis=2)
    right_rows = jax.vmap(pick_rows, in_axes=(0, 0, 0, None))(payload, border[:, 1], border_count[:, 1], 0)
    left_rows = jax.vmap(pick_rows, in_axes=(0, 0, 0, None))(payload, border[:, 0], border_count[:, 0], 0)
    blank = jnp.zeros_like(right_rows[:1])
    from_left = jnp.concatenate([blank, right_rows[:-1]], axis=0)
    from_right = jnp.concatenate([left_rows[1:], blank], axis=0)
    extended = jnp.concatenate([payload, from_left, from_right], axis=1)
    short_table = lax.optimization_barrier(forward_table(K, F0, BAND, NF).astype(jnp.bfloat16)).astype(jnp.float32)
    lag_table = lax.optimization_barrier(inverse_table(LN, F0, BAND, NF).astype(jnp.bfloat16)).astype(jnp.float32)

    def region_scores(region_items):
        ext_rows, region_waves, region_ids, region_moves, region_active = region_items
        ext_spectra = ext_rows[:, :2 * BAND]
        station_norm = jnp.sqrt(ext_rows[:, 2 * BAND:] + EPSILON)
        templ_total = region_waves.shape[0]
        block_size = 48 if templ_total % 48 == 0 else templ_total
        block_total = templ_total // block_size

        def run_block(block_items):
            return block_scores(block_items, ext_spectra, station_norm, short_table, lag_table)
        stacked = lax.map(run_block, (region_waves.reshape(block_total, block_size, SLOTS, K), region_ids.reshape(block_total, block_size, SLOTS), region_moves.reshape(block_total, block_size, SLOTS), region_active.reshape(block_total, block_size)))
        return stacked.reshape(templ_total, OUT)
    return lax.map(region_scores, (extended, templates, channel_ids, moveouts, active))
```

```python
import functools

import jax
import jax.numpy as jnp
import ml_dtypes
import numpy as np
from jax import lax
from jax.experimental import pallas as pl
from jax.experimental.pallas import tpu as pltpu
from jax.sharding import PartitionSpec as P

NF = 2048
F0 = 40
BAND = 384
K = 400
OUT = 512
LN = 1024
EPSILON = 1e-06

LANES = 128
RES = NF // LANES
STEPS = BAND // RES
COPIES = LANES // RES
PART = STEPS // COPIES
SPEC_ROWS = 2 * PART
BLOCKS = LN // LANES
SPAN = LN + OUT
MESH = pl.DeviceIdType.MESH
TURN = 2.0 * np.pi / NF
BF16, F32 = jnp.bfloat16, jnp.float32
ACROSS = (((1,), (1,)), ((), ()))


def as_bf16(x):
    return x.astype(np.float32).astype(ml_dtypes.bfloat16)


def halves(x):
    x = x.astype(np.float32)
    high = x.astype(ml_dtypes.bfloat16)
    return high, (x - high.astype(np.float32)).astype(ml_dtypes.bfloat16)


def bin_order():
    i, k, r = np.meshgrid(np.arange(PART), np.arange(COPIES), np.arange(RES), indexing="ij")
    return (F0 + RES * (PART * k + i) + r).reshape(-1)


def wide_tables():
    bins = bin_order()
    short = (np.arange(K)[:, None] * bins[None, :] % NF) * TURN
    short = np.concatenate([np.cos(short), -np.sin(short)], axis=1)
    lag = (bins[:, None] * np.arange(SPAN)[None, :] % NF) * TURN
    lag = np.concatenate([np.cos(lag), -np.sin(lag)], axis=0)
    return as_bf16(short), as_bf16(lag)


def small_tables(chans):
    r, a, b = np.arange(RES), np.arange(RES), np.arange(LANES)
    alpha = (F0 + r)[:, None] * a[None, :] * LANES % NF * TURN
    spread = lambda x: np.einsum("ra,cd->crad", x, np.eye(chans)).reshape(chans * RES, RES * chans)
    high, low = halves(np.concatenate([spread(np.cos(alpha)), spread(-np.sin(alpha))], axis=0))
    gather = np.concatenate([high, high, low], axis=1)
    theta = np.tile((F0 + r)[:, None] * b[None, :] % NF * TURN, (chans, 1))
    twiddle = np.concatenate([np.cos(theta), np.sin(theta)], axis=0).astype(np.float32)
    rows = np.zeros((COPIES, 8, 2 * LANES))
    for k in range(COPIES):
        beta = (PART * k + np.arange(PART))[:, None] * b[None, :] * RES % NF * TURN
        rows[k, :PART] = np.concatenate([np.cos(beta), np.sin(beta)], axis=1)
        rows[k, PART : 2 * PART] = np.concatenate([-np.sin(beta), np.cos(beta)], axis=1)
    steps = np.concatenate(halves(rows.reshape(8 * COPIES, 2 * LANES)), axis=0)
    window = []
    for i in (0, 1, 3, 4):
        place = LANES * i + b[:, None] - b[None, :]
        window.append((place >= 0) & (place < K))
    return gather, twiddle, steps, as_bf16(np.concatenate(window, axis=0))


def split(x):
    high = x.astype(BF16)
    return high, (x - high.astype(F32)).astype(BF16)


def dot(a, b):
    return jnp.dot(a, b, preferred_element_type=F32)


def kernel(geometry, spaces, bmax, *refs):
    count = len(spaces)
    hbm, out_ref, local = refs[:count], refs[count], refs[count + 1 : 2 * count + 1]
    (
        recv_ref, tspec_ref, hot_ref, weight_ref, chosen_ref, parts_ref, norms_ref, lhs_ref,
        line_ref, sums_ref, base_ref, turn_ref, load_sem, send_sem, recv_sem, go_sem,
    ) = refs[2 * count + 1 :]
    loads = [pltpu.make_async_copy(h, v, load_sem.at[i]) for i, (h, v) in enumerate(zip(hbm, local))]
    for load in loads:
        load.start()
    (
        wave_ref, gather_ref, twiddle_ref, steps_ref, border_ref, count_ref, tmpl_ref, short_ref,
        ids_ref, active_ref, move_ref, window_ref, lag_ref,
    ) = local
    regions, tmpls, subs, offsets = geometry
    group, blocks = tmpls * subs, len(offsets)
    slots_n = group * blocks
    region, tmpl, sub = (lax.axis_index(a) for a in ("region", "tmpl", "sub"))
    place = tmpl * subs + sub
    mine = (tmpl * regions + region) * subs + sub
    chans = wave_ref.shape[0] // RES
    pay_rows = chans * SPEC_ROWS + 1
    stride = -(-pay_rows // 8) * 8
    own = group * chans
    total = slots_n * chans
    slots, _, templs = ids_ref.shape
    wide = slots * templs

    def peer(index):
        there, other = index // (blocks * subs), lax.rem(index, subs)
        block = lax.rem(index // subs, blocks)
        if regions == blocks:
            far = block
            step = lax.rem(region - far + regions, regions)
            block = jnp.where(step == 0, 0, jnp.where(step == regions - 1, 1, 2))
        else:
            step = jnp.where(block == 0, 0, jnp.where(block == 1, regions - 1, 1))
            far = lax.rem(region + regions - step, regions)
        back = lax.rem(regions - step, regions)
        back = jnp.where(back == 0, 0, jnp.where(back == regions - 1, 1, 2))
        device = {"region": far, "tmpl": there, "sub": other}
        rank = (there * regions + far) * subs + other
        return device, rank, block * group + place, back * group + there * subs + other

    def each_peer(action):
        lax.fori_loop(0, slots_n, lambda i, c: (action(i, *peer(i)), c)[1], 0)

    def slot_rows(slot):
        return recv_ref.at[pl.ds(pl.multiple_of(slot * stride, 8), pay_rows), :]

    def copy_to(slot, device, lane):
        return pltpu.make_async_remote_copy(
            src_ref=slot_rows(place), dst_ref=slot_rows(slot), send_sem=send_sem.at[lane],
            recv_sem=recv_sem.at[slot], device_id=device, device_id_type=MESH,
        )

    barrier = pltpu.get_barrier_semaphore()
    lower = jnp.int32(0)

    def greet(i, below):
        device, rank, _, _ = peer(i)

        @pl.when(rank > mine)
        def _():
            pl.semaphore_signal(barrier, inc=1, device_id=device, device_id_type=MESH)

        return below + jnp.where(rank < mine, 1, 0)

    lower = lax.fori_loop(0, slots_n, greet, lower)

    @pl.when(lower > 0)
    def _():
        pl.semaphore_wait(barrier, lower)

    def announce(i, device, rank, slot, _):
        @pl.when(rank < mine)
        def _():
            pl.semaphore_signal(go_sem.at[slot], inc=1, device_id=device, device_id_type=MESH)

    each_peer(announce)

    start = pl.multiple_of(place * stride, 8)
    loads[4].wait()
    loads[5].wait()
    lane = lax.broadcasted_iota(jnp.int32, (1, LANES), 1)
    info = start + chans * SPEC_ROWS
    recv_ref[pl.ds(info, 1), :] = jnp.full((1, LANES), -1.0, F32)
    for i, side in enumerate((1, 0)):
        live = lane[:, :bmax] < count_ref[:, side : side + 1]
        listed = jnp.where(live, border_ref[side : side + 1, :], -1).astype(F32)
        recv_ref[pl.ds(info, 1), own + i * bmax : own + (i + 1) * bmax] = listed

    loads[0].wait()
    loads[1].wait()
    high, low = split(wave_ref[...])
    y = dot(gather_ref[...], jnp.concatenate([high, low, high], axis=0))
    half = RES * chans
    loads[2].wait()
    cos, sin = twiddle_ref[:half, :], twiddle_ref[half:, :]
    yr, yi = y[:half], y[half:]
    z = jnp.concatenate([yr * cos + yi * sin, yi * cos - yr * sin], axis=1)
    repeat = lambda x: jnp.concatenate(
        [x[RES * c : RES * (c + 1)] for c in range(chans) for _ in range(COPIES)], axis=0
    )
    high, low = split(z)
    loads[3].wait()
    nt = lambda a, b: lax.dot_general(a, b, ACROSS, preferred_element_type=F32)
    first = nt(steps_ref[...], repeat(high))
    x = first[: 8 * COPIES] + (first[8 * COPIES :] + nt(steps_ref[: 8 * COPIES, :], repeat(low)))
    for c in range(chans):
        piece = x[:8, LANES * c : LANES * (c + 1)]
        for k in range(1, COPIES):
            piece = jnp.where(
                lane >= RES * k, x[8 * k : 8 * (k + 1), LANES * c : LANES * (c + 1)], piece
            )
        recv_ref[pl.ds(start + c * SPEC_ROWS, SPEC_ROWS), :] = piece[:SPEC_ROWS]

    def send_down(i, device, rank, slot, _):
        @pl.when(rank < mine)
        def _():
            copy_to(slot, device, i).start()

    each_peer(send_down)

    loads[6].wait()
    loads[7].wait()
    waves = tmpl_ref[...]
    tspec_ref[...] = dot(waves, short_ref[...])
    waves = waves.astype(F32)
    power = jnp.sum(waves * waves, axis=1, keepdims=True)
    loads[8].wait()
    loads[9].wait()
    square = (templs, templs)
    same = lax.broadcasted_iota(jnp.int32, square, 0) == lax.broadcasted_iota(jnp.int32, square, 1)
    column = lambda x: jnp.sum(jnp.where(same, x, 0), axis=1, keepdims=True, dtype=jnp.int32)
    used = column(active_ref[...])
    ids = jnp.concatenate([column(ids_ref[j]) for j in range(slots)], axis=0)
    live = jnp.concatenate([jnp.where(used > j, 1.0, 0.0) for j in range(slots)], axis=0)
    one = lambda mask: jnp.where(mask, 1.0, 0.0).astype(BF16)
    hot_ref[...] = one(ids == lane)
    scale = 2.0 / NF * lax.rsqrt(power + EPSILON) * live
    scale_high = scale.astype(BF16).astype(F32)
    part = lax.broadcasted_iota(jnp.int32, (1, 3 * total), 1)
    weight_ref[...] = jnp.where(part < 2 * total, scale_high, scale - scale_high).astype(BF16)
    loads[10].wait()

    def places(j, carry):
        for t in range(templs):
            move = move_ref[j, 0, t]
            base_ref[j * templs + t] = (j * templs + t) * BLOCKS + (move >> 7)
            turn_ref[j * templs + t] = move & (LANES - 1)
        return carry

    lax.fori_loop(0, slots, places, 0)

    def send_up(i, device, rank, slot, back):
        @pl.when(rank > mine)
        def _():
            pl.semaphore_wait(go_sem.at[back], 1)
            copy_to(slot, device, i).start()

    each_peer(send_up)

    left = offsets.index((regions - 1) % regions)
    right = offsets.index(1 % regions)
    far = sorted({b for b in (left, right) if b})
    for b in far:
        copy_to(b * group + place, {"sub": sub}, 0).wait_recv()
    listed = lambda b: recv_ref[pl.ds(pl.multiple_of((b * group + place) * stride, 8) + chans * SPEC_ROWS, 1), :].astype(jnp.int32)

    def row_of(b, channel):
        row = lax.rem(channel, chans) * slots_n + b * group + channel // chans
        return jnp.where(channel < 0, -1, row)

    from_left = jnp.where(region > 0, row_of(left, listed(left)), -1)
    from_right = jnp.where(region < regions - 1, row_of(right, listed(right)), -1)
    target = jnp.where(
        lane < own, row_of(0, lane), jnp.where(lane < own + bmax, from_left, from_right)
    )
    row = lax.rem(lax.broadcasted_iota(jnp.int32, (3 * total, 1), 0), total)
    chosen = lax.dot_general(hot_ref[...], one(row == target), ACROSS, preferred_element_type=F32)
    chosen_ref[...] = chosen.astype(BF16)
    weight_ref[...] = (chosen * weight_ref[...].astype(F32)).astype(BF16)
    loads[11].wait()
    loads[12].wait()

    def arrive(i, device, rank, slot, back):
        skip = rank == mine
        for b in far:
            skip = skip | (back == b * group + place)

        @pl.when(jnp.logical_not(skip))
        def _():
            copy_to(back, device, 0).wait_recv()

    each_peer(arrive)

    table = jnp.concatenate(
        [
            jnp.concatenate(
                [
                    recv_ref[pl.ds(c * SPEC_ROWS + i, slots_n, stride=stride), :]
                    for i in range(SPEC_ROWS)
                ],
                axis=1,
            )
            for c in range(chans)
        ],
        axis=0,
    )
    high = table.astype(BF16)
    rest = table - high.astype(F32)
    middle, low = split(rest)
    parts_ref[...] = jnp.concatenate([high, middle, low], axis=0)
    filtered = 2.0 / NF * dot(high, lag_ref[...])
    power = filtered * filtered
    block = lambda i: power[:, LANES * i : LANES * (i + 1)]
    pieces = jnp.concatenate(
        [
            jnp.concatenate([block(q), block(q + 1) + block(q + 2), block(q + 3), block(q + 4)], axis=1)
            for q in range(BLOCKS)
        ],
        axis=0,
    )
    energy = dot(pieces.astype(BF16), window_ref[...])
    high, middle = split(lax.rsqrt(energy + EPSILON))
    for q in range(BLOCKS):
        at = slice(LANES * q, LANES * (q + 1))
        norms_ref[:total, at] = high[total * q : total * (q + 1)]
        norms_ref[total : 2 * total, at] = middle[total * q : total * (q + 1)]
        norms_ref[2 * total :, at] = high[total * q : total * (q + 1)]

    spec = dot(chosen_ref[...], parts_ref[...])
    xr, xi = spec[:, :BAND], spec[:, BAND:]
    wr, wi = tspec_ref[:, :BAND], tspec_ref[:, BAND:]
    lhs_ref[:, :BAND] = (wr * xr + wi * xi).astype(BF16)
    lhs_ref[:, BAND:] = (wr * xi - wi * xr).astype(BF16)
    step = 2 * LANES
    for c in range(0, LN, step):
        corr = dot(lhs_ref[...], lag_ref[:, c : c + step])
        normed = corr * dot(weight_ref[...], norms_ref[:, c : c + step])
        for k in range(step // LANES):
            line_ref[pl.ds(c // LANES + k, wide, stride=BLOCKS), :] = normed[
                :, LANES * k : LANES * (k + 1)
            ]

    rows_out = OUT // LANES
    lane4 = lax.broadcasted_iota(jnp.int32, (rows_out, LANES), 1)

    def one_template(t, carry):
        score = jnp.zeros((rows_out, LANES), F32)
        for j in range(slots):
            at, turn = base_ref[j * templs + t], turn_ref[j * templs + t]
            near = line_ref[pl.ds(at, rows_out), :]
            next_ = line_ref[pl.ds(at + 1, rows_out), :]
            joined = jnp.where(lane4 >= turn, near, next_)
            score += pltpu.roll(joined, (LANES - turn) & (LANES - 1), 1)
        sums_ref[pl.ds(t * rows_out, rows_out), :] = score
        return carry

    lax.fori_loop(0, templs, one_template, 0, unroll=8)
    for a in range(rows_out):
        out_ref[:, LANES * a : LANES * (a + 1)] = sums_ref[pl.ds(a, templs, stride=rows_out), :]

    def sent(i, device, rank, slot, _):
        @pl.when(rank != mine)
        def _():
            copy_to(slot, device, i).wait_send()

    each_peer(sent)


def on_device(geometry, waveforms, templates, channel_ids, moveouts, active, border, border_count):
    regions, tmpls, subs, offsets = geometry
    slots_n = tmpls * subs * len(offsets)
    chans = waveforms.shape[1]
    bmax = border.shape[2]
    templs, slots = channel_ids.shape[1:]
    wide, total = slots * templs, slots_n * chans
    by_slot = lambda x: jnp.transpose(x, (2, 0, 1))
    short_table, lag_table = wide_tables()
    gather, twiddle, steps, window = small_tables(chans)
    waves = waveforms[0].reshape(chans, RES, LANES).swapaxes(0, 1).reshape(RES * chans, LANES)
    rows = jnp.swapaxes(templates[0], 0, 1).reshape(wide, K)
    inputs = (
        waves, gather, twiddle, steps, border[0], border_count, rows, short_table,
        by_slot(channel_ids), active, by_slot(moveouts), window, lag_table,
    )
    spaces = [pltpu.SMEM if i == 10 else pltpu.VMEM for i in range(len(inputs))]
    stride = -(-(chans * SPEC_ROWS + 1) // 8) * 8
    vmem = pltpu.VMEM
    scores = pl.pallas_call(
        functools.partial(kernel, geometry, spaces, bmax),
        out_shape=pltpu.VMEM((templs, OUT), F32),
        in_specs=[pl.BlockSpec(memory_space=pltpu.HBM)] * len(inputs),
        out_specs=pl.BlockSpec(memory_space=pltpu.VMEM),
        scratch_shapes=[
            *[space(x.shape, x.dtype) for space, x in zip(spaces, inputs)],
            vmem((slots_n * stride, LANES), F32),
            vmem((wide, 2 * BAND), F32),
            vmem((wide, LANES), BF16),
            vmem((wide, 3 * total), BF16),
            vmem((wide, 3 * total), BF16),
            vmem((3 * total, 2 * BAND), BF16),
            vmem((3 * total, LN), BF16),
            vmem((wide, 2 * BAND), BF16),
            vmem((wide * BLOCKS + 8, LANES), F32),
            vmem((templs * (OUT // LANES), LANES), F32),
            pltpu.SMEM((wide,), jnp.int32),
            pltpu.SMEM((wide,), jnp.int32),
            pltpu.SemaphoreType.DMA((len(inputs),)),
            pltpu.SemaphoreType.DMA((slots_n,)),
            pltpu.SemaphoreType.DMA((slots_n,)),
            pltpu.SemaphoreType.REGULAR((slots_n,)),
        ],
        compiler_params=pltpu.CompilerParams(
            collective_id=0, has_side_effects=True
        ),
        name="detect",
    )(*inputs)
    return scores[None]


def solution(mesh):
    regions, tmpls, subs = (mesh.shape[a] for a in ("region", "tmpl", "sub"))
    offsets = tuple(dict.fromkeys((0, (regions - 1) % regions, 1 % regions)))
    geometry = (regions, tmpls, subs, offsets)
    in_specs = (
        P("region", ("tmpl", "sub"), "groups"),
        P("region", ("tmpl", "sub"), None, None),
        P("region", ("tmpl", "sub"), None),
        P("region", ("tmpl", "sub"), None),
        P("region", ("tmpl", "sub")),
        P("region", None, None),
        P("region", None),
    )
    return jax.shard_map(
        functools.partial(on_device, geometry),
        mesh=mesh,
        in_specs=in_specs,
        out_specs=P("region", ("tmpl", "sub"), "groups"),
        check_vma=False,
    )
```

```python
import functools

import jax
import jax.numpy as jnp
import ml_dtypes
import numpy as np
from jax import lax
from jax.experimental import pallas as pl
from jax.experimental.pallas import tpu as pltpu
from jax.sharding import PartitionSpec as P

NF = 2048
F0 = 40
BAND = 384
K = 400
OUT = 512
LN = 1024
EPSILON = 1e-06

LANES = 128
RES = NF // LANES
STEPS = BAND // RES
COPIES = LANES // RES
PART = STEPS // COPIES
SPEC_ROWS = 2 * PART
BLOCKS = LN // LANES
SPAN = LN + OUT
MESH = pl.DeviceIdType.MESH
TURN = 2.0 * np.pi / NF
BF16, F32 = jnp.bfloat16, jnp.float32
ACROSS = (((1,), (1,)), ((), ()))


def as_bf16(x):
    return x.astype(np.float32).astype(ml_dtypes.bfloat16)


def halves(x):
    x = x.astype(np.float32)
    high = x.astype(ml_dtypes.bfloat16)
    return high, (x - high.astype(np.float32)).astype(ml_dtypes.bfloat16)


def bin_order():
    i, k, r = np.meshgrid(np.arange(PART), np.arange(COPIES), np.arange(RES), indexing="ij")
    return (F0 + RES * (PART * k + i) + r).reshape(-1)


def wide_tables():
    bins = bin_order()
    short = (np.arange(K)[:, None] * bins[None, :] % NF) * TURN
    short = np.concatenate([np.cos(short), -np.sin(short)], axis=1)
    lag = (bins[:, None] * np.arange(SPAN)[None, :] % NF) * TURN
    lag = np.concatenate([np.cos(lag), -np.sin(lag)], axis=0)
    return as_bf16(short), as_bf16(lag)


def small_tables(chans):
    r, a, b = np.arange(RES), np.arange(RES), np.arange(LANES)
    alpha = (F0 + r)[:, None] * a[None, :] * LANES % NF * TURN
    spread = lambda x: np.einsum("ra,cd->crad", x, np.eye(chans)).reshape(chans * RES, RES * chans)
    high, low = halves(np.concatenate([spread(np.cos(alpha)), spread(-np.sin(alpha))], axis=0))
    gather = np.concatenate([high, high, low], axis=1)
    theta = np.tile((F0 + r)[:, None] * b[None, :] % NF * TURN, (chans, 1))
    twiddle = np.concatenate([np.cos(theta), np.sin(theta)], axis=0).astype(np.float32)
    rows = np.zeros((COPIES, 8, 2 * LANES))
    for k in range(COPIES):
        beta = (PART * k + np.arange(PART))[:, None] * b[None, :] * RES % NF * TURN
        rows[k, :PART] = np.concatenate([np.cos(beta), np.sin(beta)], axis=1)
        rows[k, PART : 2 * PART] = np.concatenate([-np.sin(beta), np.cos(beta)], axis=1)
    steps = np.concatenate(halves(rows.reshape(8 * COPIES, 2 * LANES)), axis=0)
    window = []
    for i in (0, 1, 3, 4):
        place = LANES * i + b[:, None] - b[None, :]
        window.append((place >= 0) & (place < K))
    return gather, twiddle, steps, as_bf16(np.concatenate(window, axis=0))


def split(x):
    high = x.astype(BF16)
    return high, (x - high.astype(F32)).astype(BF16)


def dot(a, b):
    return jnp.dot(a, b, preferred_element_type=F32)


def kernel(geometry, spaces, bmax, *refs):
    count = len(spaces)
    hbm, out_ref, local = refs[:count], refs[count], refs[count + 1 : 2 * count + 1]
    (
        recv_ref, tspec_ref, hot_ref, weight_ref, chosen_ref, parts_ref, norms_ref, lhs_ref,
        line_ref, sums_ref, base_ref, turn_ref, load_sem, send_sem, recv_sem, go_sem,
    ) = refs[2 * count + 1 :]
    loads = [pltpu.make_async_copy(h, v, load_sem.at[i]) for i, (h, v) in enumerate(zip(hbm, local))]
    for load in loads:
        load.start()
    (
        wave_ref, gather_ref, twiddle_ref, steps_ref, border_ref, count_ref, tmpl_ref, short_ref,
        ids_ref, active_ref, move_ref, window_ref, lag_ref,
    ) = local
    regions, tmpls, subs, offsets = geometry
    group, blocks = tmpls * subs, len(offsets)
    slots_n = group * blocks
    region, tmpl, sub = (lax.axis_index(a) for a in ("region", "tmpl", "sub"))
    place = tmpl * subs + sub
    mine = (tmpl * regions + region) * subs + sub
    chans = wave_ref.shape[0] // RES
    pay_rows = chans * SPEC_ROWS + 1
    stride = -(-pay_rows // 8) * 8
    own = group * chans
    total = slots_n * chans
    slots, _, templs = ids_ref.shape
    wide = slots * templs

    def peer(index):
        there, other = index // (blocks * subs), index % subs
        block = index // subs % blocks
        if regions == blocks:
            far = block
            step = lax.rem(region - far + regions, regions)
            block = jnp.where(step == 0, 0, jnp.where(step == regions - 1, 1, 2))
        else:
            step = (0, regions - 1, 1)[block]
            far = lax.rem(region + regions - step, regions)
        back = lax.rem(regions - step, regions)
        back = jnp.where(back == 0, 0, jnp.where(back == regions - 1, 1, 2))
        device = {"region": far, "tmpl": there, "sub": other}
        rank = (there * regions + far) * subs + other
        twin = jnp.where((there == tmpl) & (other == sub), block, 0)
        return device, rank, block * group + place, back * group + there * subs + other, twin

    def each_peer(action):
        for i in range(slots_n):
            action(*peer(i))

    def slot_rows(slot):
        return recv_ref.at[pl.ds(pl.multiple_of(slot * stride, 8), pay_rows), :]

    def copy_to(slot, device, lane):
        return pltpu.make_async_remote_copy(
            src_ref=slot_rows(place), dst_ref=slot_rows(slot), send_sem=send_sem,
            recv_sem=recv_sem.at[lane], device_id=device, device_id_type=MESH,
        )

    def rows_of(copies):
        return recv_ref.at[pl.ds(0, copies * pay_rows), :]

    barrier = pltpu.get_barrier_semaphore()
    lower = jnp.int32(0)
    for i in range(slots_n):
        device, rank = peer(i)[:2]

        @pl.when(rank > mine)
        def _():
            pl.semaphore_signal(barrier, inc=1, device_id=device, device_id_type=MESH)

        lower += jnp.where(rank < mine, 1, 0)

    @pl.when(lower > 0)
    def _():
        pl.semaphore_wait(barrier, lower)

    def announce(device, rank, slot, back, twin):
        @pl.when(rank < mine)
        def _():
            pl.semaphore_signal(go_sem.at[slot], inc=1, device_id=device, device_id_type=MESH)

    each_peer(announce)

    start = pl.multiple_of(place * stride, 8)
    loads[4].wait()
    loads[5].wait()
    lane = lax.broadcasted_iota(jnp.int32, (1, LANES), 1)
    info = start + chans * SPEC_ROWS
    recv_ref[pl.ds(info, 1), :] = jnp.full((1, LANES), -1.0, F32)
    for i, side in enumerate((1, 0)):
        live = lane[:, :bmax] < count_ref[:, side : side + 1]
        listed = jnp.where(live, border_ref[side : side + 1, :], -1).astype(F32)
        recv_ref[pl.ds(info, 1), own + i * bmax : own + (i + 1) * bmax] = listed

    loads[0].wait()
    loads[1].wait()
    high, low = split(wave_ref[...])
    y = dot(gather_ref[...], jnp.concatenate([high, low, high], axis=0))
    half = RES * chans
    loads[2].wait()
    cos, sin = twiddle_ref[:half, :], twiddle_ref[half:, :]
    yr, yi = y[:half], y[half:]
    z = jnp.concatenate([yr * cos + yi * sin, yi * cos - yr * sin], axis=1)
    repeat = lambda x: jnp.concatenate(
        [x[RES * c : RES * (c + 1)] for c in range(chans) for _ in range(COPIES)], axis=0
    )
    high, low = split(z)
    loads[3].wait()
    nt = lambda a, b: lax.dot_general(a, b, ACROSS, preferred_element_type=F32)
    first = nt(steps_ref[...], repeat(high))
    x = first[: 8 * COPIES] + (first[8 * COPIES :] + nt(steps_ref[: 8 * COPIES, :], repeat(low)))
    for c in range(chans):
        piece = x[:8, LANES * c : LANES * (c + 1)]
        for k in range(1, COPIES):
            piece = jnp.where(
                lane >= RES * k, x[8 * k : 8 * (k + 1), LANES * c : LANES * (c + 1)], piece
            )
        recv_ref[pl.ds(start + c * SPEC_ROWS, SPEC_ROWS), :] = piece[:SPEC_ROWS]

    def send_down(device, rank, slot, back, twin):
        @pl.when(rank < mine)
        def _():
            copy_to(slot, device, twin).start()

    each_peer(send_down)

    loads[6].wait()
    loads[7].wait()
    waves = tmpl_ref[...]
    tspec_ref[...] = dot(waves, short_ref[...])
    waves = waves.astype(F32)
    power = jnp.sum(waves * waves, axis=1, keepdims=True)
    loads[8].wait()
    loads[9].wait()
    square = (templs, templs)
    same = lax.broadcasted_iota(jnp.int32, square, 0) == lax.broadcasted_iota(jnp.int32, square, 1)
    column = lambda x: jnp.sum(jnp.where(same, x, 0), axis=1, keepdims=True, dtype=jnp.int32)
    used = column(active_ref[...])
    ids = jnp.concatenate([column(ids_ref[j]) for j in range(slots)], axis=0)
    live = jnp.concatenate([jnp.where(used > j, 1.0, 0.0) for j in range(slots)], axis=0)
    one = lambda mask: jnp.where(mask, 1.0, 0.0).astype(BF16)
    hot_ref[...] = one(ids == lane)
    scale = 2.0 / NF * lax.rsqrt(power + EPSILON) * live
    scale_high = scale.astype(BF16).astype(F32)
    part = lax.broadcasted_iota(jnp.int32, (1, 3 * total), 1)
    weight_ref[...] = jnp.where(part < 2 * total, scale_high, scale - scale_high).astype(BF16)
    loads[10].wait()

    def places(j, carry):
        for t in range(templs):
            move = move_ref[j, 0, t]
            base_ref[j * templs + t] = (j * templs + t) * BLOCKS + (move >> 7)
            turn_ref[j * templs + t] = move & (LANES - 1)
        return carry

    lax.fori_loop(0, slots, places, 0)

    def send_up(device, rank, slot, back, twin):
        @pl.when(rank > mine)
        def _():
            pl.semaphore_wait(go_sem.at[back], 1)
            copy_to(slot, device, twin).start()

    each_peer(send_up)

    left = offsets.index((regions - 1) % regions)
    right = offsets.index(1 % regions)
    far = sorted({b for b in (left, right) if b})
    for b in far:
        copy_to(b * group + place, {"sub": sub}, b).wait_recv()
    listed = lambda b: recv_ref[pl.ds(pl.multiple_of((b * group + place) * stride, 8) + chans * SPEC_ROWS, 1), :].astype(jnp.int32)

    def row_of(b, channel):
        row = lax.rem(channel, chans) * slots_n + b * group + channel // chans
        return jnp.where(channel < 0, -1, row)

    from_left = jnp.where(region > 0, row_of(left, listed(left)), -1)
    from_right = jnp.where(region < regions - 1, row_of(right, listed(right)), -1)
    target = jnp.where(
        lane < own, row_of(0, lane), jnp.where(lane < own + bmax, from_left, from_right)
    )
    row = lax.rem(lax.broadcasted_iota(jnp.int32, (3 * total, 1), 0), total)
    chosen = lax.dot_general(hot_ref[...], one(row == target), ACROSS, preferred_element_type=F32)
    chosen_ref[...] = chosen.astype(BF16)
    weight_ref[...] = (chosen * weight_ref[...].astype(F32)).astype(BF16)
    loads[11].wait()
    loads[12].wait()

    others = rows_of(slots_n - 1 - len(far))
    pltpu.make_async_copy(others, others, recv_sem.at[0]).wait()

    table = jnp.concatenate(
        [
            jnp.concatenate(
                [
                    recv_ref[pl.ds(c * SPEC_ROWS + i, slots_n, stride=stride), :]
                    for i in range(SPEC_ROWS)
                ],
                axis=1,
            )
            for c in range(chans)
        ],
        axis=0,
    )
    high = table.astype(BF16)
    rest = table - high.astype(F32)
    middle, low = split(rest)
    parts_ref[...] = jnp.concatenate([high, middle, low], axis=0)
    filtered = 2.0 / NF * dot(high, lag_ref[...])
    power = filtered * filtered
    block = lambda i: power[:, LANES * i : LANES * (i + 1)]
    pieces = jnp.concatenate(
        [
            jnp.concatenate([block(q), block(q + 1) + block(q + 2), block(q + 3), block(q + 4)], axis=1)
            for q in range(BLOCKS)
        ],
        axis=0,
    )
    energy = dot(pieces.astype(BF16), window_ref[...])
    high, middle = split(lax.rsqrt(energy + EPSILON))
    for q in range(BLOCKS):
        at = slice(LANES * q, LANES * (q + 1))
        norms_ref[:total, at] = high[total * q : total * (q + 1)]
        norms_ref[total : 2 * total, at] = middle[total * q : total * (q + 1)]
        norms_ref[2 * total :, at] = high[total * q : total * (q + 1)]

    spec = dot(chosen_ref[...], parts_ref[...])
    xr, xi = spec[:, :BAND], spec[:, BAND:]
    wr, wi = tspec_ref[:, :BAND], tspec_ref[:, BAND:]
    lhs_ref[:, :BAND] = (wr * xr + wi * xi).astype(BF16)
    lhs_ref[:, BAND:] = (wr * xi - wi * xr).astype(BF16)
    step = 2 * LANES
    for c in range(0, LN, step):
        corr = dot(lhs_ref[...], lag_ref[:, c : c + step])
        normed = corr * dot(weight_ref[...], norms_ref[:, c : c + step])
        for k in range(step // LANES):
            line_ref[pl.ds(c // LANES + k, wide, stride=BLOCKS), :] = normed[
                :, LANES * k : LANES * (k + 1)
            ]

    rows_out = OUT // LANES
    lane4 = lax.broadcasted_iota(jnp.int32, (rows_out, LANES), 1)

    def one_template(t, carry):
        score = jnp.zeros((rows_out, LANES), F32)
        for j in range(slots):
            at, turn = base_ref[j * templs + t], turn_ref[j * templs + t]
            near = line_ref[pl.ds(at, rows_out), :]
            next_ = line_ref[pl.ds(at + 1, rows_out), :]
            joined = jnp.where(lane4 >= turn, near, next_)
            score += pltpu.roll(joined, (LANES - turn) & (LANES - 1), 1)
        sums_ref[pl.ds(t * rows_out, rows_out), :] = score
        return carry

    lax.fori_loop(0, templs, one_template, 0, unroll=8)
    for a in range(rows_out):
        out_ref[:, LANES * a : LANES * (a + 1)] = sums_ref[pl.ds(a, templs, stride=rows_out), :]

    others = rows_of(slots_n - 1)
    pltpu.make_async_copy(others, others, send_sem).wait()


def on_device(geometry, waveforms, templates, channel_ids, moveouts, active, border, border_count):
    regions, tmpls, subs, offsets = geometry
    slots_n = tmpls * subs * len(offsets)
    chans = waveforms.shape[1]
    bmax = border.shape[2]
    templs, slots = channel_ids.shape[1:]
    wide, total = slots * templs, slots_n * chans
    by_slot = lambda x: jnp.transpose(x, (2, 0, 1))
    short_table, lag_table = wide_tables()
    gather, twiddle, steps, window = small_tables(chans)
    waves = waveforms[0].reshape(chans, RES, LANES).swapaxes(0, 1).reshape(RES * chans, LANES)
    rows = jnp.swapaxes(templates[0], 0, 1).reshape(wide, K)
    inputs = (
        waves, gather, twiddle, steps, border[0], border_count, rows, short_table,
        by_slot(channel_ids), active, by_slot(moveouts), window, lag_table,
    )
    spaces = [pltpu.SMEM if i == 10 else pltpu.VMEM for i in range(len(inputs))]
    stride = -(-(chans * SPEC_ROWS + 1) // 8) * 8
    vmem = pltpu.VMEM
    scores = pl.pallas_call(
        functools.partial(kernel, geometry, spaces, bmax),
        out_shape=pltpu.VMEM((templs, OUT), F32),
        in_specs=[pl.BlockSpec(memory_space=pltpu.HBM)] * len(inputs),
        out_specs=pl.BlockSpec(memory_space=pltpu.VMEM),
        scratch_shapes=[
            *[space(x.shape, x.dtype) for space, x in zip(spaces, inputs)],
            vmem((slots_n * stride, LANES), F32),
            vmem((wide, 2 * BAND), F32),
            vmem((wide, LANES), BF16),
            vmem((wide, 3 * total), BF16),
            vmem((wide, 3 * total), BF16),
            vmem((3 * total, 2 * BAND), BF16),
            vmem((3 * total, LN), BF16),
            vmem((wide, 2 * BAND), BF16),
            vmem((wide * BLOCKS + 8, LANES), F32),
            vmem((templs * (OUT // LANES), LANES), F32),
            pltpu.SMEM((wide,), jnp.int32),
            pltpu.SMEM((wide,), jnp.int32),
            pltpu.SemaphoreType.DMA((len(inputs),)),
            pltpu.SemaphoreType.DMA,
            pltpu.SemaphoreType.DMA((len(offsets),)),
            pltpu.SemaphoreType.REGULAR((slots_n,)),
        ],
        compiler_params=pltpu.CompilerParams(
            collective_id=0, has_side_effects=True
        ),
        name="detect",
    )(*inputs)
    return scores[None]


def solution(mesh):
    regions, tmpls, subs = (mesh.shape[a] for a in ("region", "tmpl", "sub"))
    offsets = tuple(dict.fromkeys((0, (regions - 1) % regions, 1 % regions)))
    geometry = (regions, tmpls, subs, offsets)
    in_specs = (
        P("region", ("tmpl", "sub"), "groups"),
        P("region", ("tmpl", "sub"), None, None),
        P("region", ("tmpl", "sub"), None),
        P("region", ("tmpl", "sub"), None),
        P("region", ("tmpl", "sub")),
        P("region", None, None),
        P("region", None),
    )
    return jax.shard_map(
        functools.partial(on_device, geometry),
        mesh=mesh,
        in_specs=in_specs,
        out_specs=P("region", ("tmpl", "sub"), "groups"),
        check_vma=False,
    )
```

```python
import functools

import jax
import jax.numpy as jnp
import ml_dtypes
import numpy as np
from jax import lax
from jax.experimental import pallas as pl
from jax.experimental.pallas import tpu as pltpu
from jax.sharding import PartitionSpec as P

NF = 2048
F0 = 40
BAND = 384
K = 400
OUT = 512
LN = 1024
EPSILON = 1e-06

LANES = 128
RES = NF // LANES
STEPS = BAND // RES
COPIES = LANES // RES
PART = STEPS // COPIES
SPEC_ROWS = 2 * PART
BLOCKS = LN // LANES
SPAN = LN + OUT
MESH = pl.DeviceIdType.MESH
TURN = 2.0 * np.pi / NF
BF16, F32 = jnp.bfloat16, jnp.float32
ACROSS = (((1,), (1,)), ((), ()))


def as_bf16(x):
    return x.astype(np.float32).astype(ml_dtypes.bfloat16)


def halves(x):
    x = x.astype(np.float32)
    high = x.astype(ml_dtypes.bfloat16)
    return high, (x - high.astype(np.float32)).astype(ml_dtypes.bfloat16)


def bin_order():
    i, k, r = np.meshgrid(np.arange(PART), np.arange(COPIES), np.arange(RES), indexing="ij")
    return (F0 + RES * (PART * k + i) + r).reshape(-1)


def wide_tables():
    bins = bin_order()
    short = (np.arange(K)[:, None] * bins[None, :] % NF) * TURN
    short = np.concatenate([np.cos(short), -np.sin(short)], axis=1)
    lag = (bins[:, None] * np.arange(SPAN)[None, :] % NF) * TURN
    lag = np.concatenate([np.cos(lag), -np.sin(lag)], axis=0)
    return as_bf16(short), as_bf16(lag)


def small_tables(chans):
    r, a, b = np.arange(RES), np.arange(RES), np.arange(LANES)
    alpha = (F0 + r)[:, None] * a[None, :] * LANES % NF * TURN
    spread = lambda x: np.einsum("ra,cd->crad", x, np.eye(chans)).reshape(chans * RES, RES * chans)
    high, low = halves(np.concatenate([spread(np.cos(alpha)), spread(-np.sin(alpha))], axis=0))
    gather = np.concatenate([high, high, low], axis=1)
    theta = np.tile((F0 + r)[:, None] * b[None, :] % NF * TURN, (chans, 1))
    twiddle = np.concatenate([np.cos(theta), np.sin(theta)], axis=0).astype(np.float32)
    rows = np.zeros((COPIES, 8, 2 * LANES))
    for k in range(COPIES):
        beta = (PART * k + np.arange(PART))[:, None] * b[None, :] * RES % NF * TURN
        rows[k, :PART] = np.concatenate([np.cos(beta), np.sin(beta)], axis=1)
        rows[k, PART : 2 * PART] = np.concatenate([-np.sin(beta), np.cos(beta)], axis=1)
    steps = np.concatenate(halves(rows.reshape(8 * COPIES, 2 * LANES)), axis=0)
    window = []
    for i in (0, 1, 3, 4):
        place = LANES * i + b[:, None] - b[None, :]
        window.append((place >= 0) & (place < K))
    return gather, twiddle, steps, as_bf16(np.concatenate(window, axis=0))


def split(x):
    high = x.astype(BF16)
    return high, (x - high.astype(F32)).astype(BF16)


def dot(a, b):
    return jnp.dot(a, b, preferred_element_type=F32)


def kernel(geometry, spaces, bmax, *refs):
    count = len(spaces)
    hbm, out_ref, local = refs[:count], refs[count], refs[count + 1 : 2 * count + 1]
    (
        recv_ref, tspec_ref, hot_ref, weight_ref, chosen_ref, parts_ref, norms_ref, lhs_ref,
        *line_refs, sums_ref, words_ref, table_ref, load_sem, send_sem, recv_sem, go_sem,
    ) = refs[2 * count + 1 :]
    loads = [pltpu.make_async_copy(h, v, load_sem.at[i]) for i, (h, v) in enumerate(zip(hbm, local))]
    for load in loads:
        load.start()
    (
        wave_ref, gather_ref, twiddle_ref, steps_ref, border_ref, count_ref, tmpl_ref, short_ref,
        ids_ref, active_ref, move_ref, window_ref, lag_ref,
    ) = local
    regions, tmpls, subs, offsets = geometry
    group, blocks = tmpls * subs, len(offsets)
    slots_n = group * blocks
    region, tmpl, sub = (lax.axis_index(a) for a in ("region", "tmpl", "sub"))
    place = tmpl * subs + sub

    def rank_of(far, there, other):
        along = (there - 1) * (1 - far % 2) + (tmpls - 1 - there) * (far % 2)
        late = regions + far * (tmpls - 1) + along
        return jnp.where(there == 0, far, late) * subs + other

    mine = rank_of(region, tmpl, sub)
    chans = wave_ref.shape[0] // RES
    pay_rows = chans * SPEC_ROWS + 1
    stride = -(-pay_rows // 8) * 8
    own = group * chans
    total = slots_n * chans
    slots, _, templs = ids_ref.shape
    words = words_ref.shape[0] // 3
    wide = slots * templs

    def peer(index):
        there, other = index // (blocks * subs), index % subs
        block = index // subs % blocks
        if regions == blocks:
            far = block
            step = lax.rem(region - far + regions, regions)
            block = jnp.where(step == 0, 0, jnp.where(step == regions - 1, 1, 2))
        else:
            step = (0, regions - 1, 1)[block]
            far = lax.rem(region + regions - step, regions)
        back = lax.rem(regions - step, regions)
        back = jnp.where(back == 0, 0, jnp.where(back == regions - 1, 1, 2))
        device = {"region": far, "tmpl": there, "sub": other}
        rank = rank_of(far, there, other)
        twin = jnp.where((there == tmpl) & (other == sub), block, 0)
        return device, rank, block * group + place, back * group + there * subs + other, twin

    def each_peer(action):
        for i in range(slots_n):
            action(*peer(i))

    def slot_rows(slot):
        return recv_ref.at[pl.ds(pl.multiple_of(slot * stride, 8), pay_rows), :]

    def copy_to(slot, device, lane):
        return pltpu.make_async_remote_copy(
            src_ref=slot_rows(place), dst_ref=slot_rows(slot), send_sem=send_sem,
            recv_sem=recv_sem.at[lane], device_id=device, device_id_type=MESH,
        )

    def rows_of(copies):
        return recv_ref.at[pl.ds(0, copies * pay_rows), :]

    barrier = pltpu.get_barrier_semaphore()
    lower = jnp.int32(0)
    for i in range(slots_n):
        device, rank = peer(i)[:2]

        @pl.when(rank > mine)
        def _():
            pl.semaphore_signal(barrier, inc=1, device_id=device, device_id_type=MESH)

        lower += jnp.where(rank < mine, 1, 0)

    start = pl.multiple_of(place * stride, 8)
    loads[4].wait()
    loads[5].wait()
    lane = lax.broadcasted_iota(jnp.int32, (1, LANES), 1)
    info = start + chans * SPEC_ROWS
    recv_ref[pl.ds(info, 1), :] = jnp.full((1, LANES), -1.0, F32)
    for i, side in enumerate((1, 0)):
        live = lane[:, :bmax] < count_ref[:, side : side + 1]
        listed = jnp.where(live, border_ref[side : side + 1, :], -1).astype(F32)
        recv_ref[pl.ds(info, 1), own + i * bmax : own + (i + 1) * bmax] = listed

    loads[0].wait()
    loads[1].wait()
    high, low = split(wave_ref[...])
    y = dot(gather_ref[...], jnp.concatenate([high, low, high], axis=0))
    half = RES * chans
    loads[2].wait()
    cos, sin = twiddle_ref[:half, :], twiddle_ref[half:, :]
    yr, yi = y[:half], y[half:]
    z = jnp.concatenate([yr * cos + yi * sin, yi * cos - yr * sin], axis=1)
    repeat = lambda x: jnp.concatenate(
        [x[RES * c : RES * (c + 1)] for c in range(chans) for _ in range(COPIES)], axis=0
    )
    high, low = split(z)
    loads[3].wait()
    nt = lambda a, b: lax.dot_general(a, b, ACROSS, preferred_element_type=F32)
    first = nt(steps_ref[...], repeat(high))
    x = first[: 8 * COPIES] + (first[8 * COPIES :] + nt(steps_ref[: 8 * COPIES, :], repeat(low)))
    for c in range(chans):
        piece = x[:8, LANES * c : LANES * (c + 1)]
        for k in range(1, COPIES):
            piece = jnp.where(
                lane >= RES * k, x[8 * k : 8 * (k + 1), LANES * c : LANES * (c + 1)], piece
            )
        recv_ref[pl.ds(start + c * SPEC_ROWS, SPEC_ROWS), :] = piece[:SPEC_ROWS]

    @pl.when(lower > 0)
    def _():
        pl.semaphore_wait(barrier, lower)

    def send_down(device, rank, slot, back, twin):
        @pl.when(rank < mine)
        def _():
            copy_to(slot, device, twin).start()

    each_peer(send_down)

    def announce(device, rank, slot, back, twin):
        @pl.when(rank < mine)
        def _():
            pl.semaphore_signal(go_sem.at[slot], inc=1, device_id=device, device_id_type=MESH)

    each_peer(announce)

    loads[6].wait()
    loads[7].wait()
    waves = tmpl_ref[...]
    tspec_ref[...] = dot(waves, short_ref[...])
    waves = waves.astype(F32)
    power = jnp.sum(waves * waves, axis=1, keepdims=True)
    loads[8].wait()
    loads[9].wait()
    square = (templs, templs)
    same = lax.broadcasted_iota(jnp.int32, square, 0) == lax.broadcasted_iota(jnp.int32, square, 1)
    column = lambda x: jnp.sum(jnp.where(same, x, 0), axis=1, keepdims=True, dtype=jnp.int32)
    used = column(active_ref[...])
    id_rows = jnp.concatenate([column(ids_ref[j]) for j in range(slots)], axis=0)
    live = jnp.concatenate([jnp.where(used > j, 1.0, 0.0) for j in range(slots)], axis=0)
    one = lambda mask: jnp.where(mask, 1.0, 0.0).astype(BF16)
    hot_ref[...] = one(id_rows == lane)
    scale = 2.0 / NF * lax.rsqrt(power + EPSILON) * live
    weight_ref[...] = jnp.broadcast_to(scale, (wide, LANES))
    ids = jnp.concatenate([ids_ref[j] for j in range(slots)], axis=0)
    loads[10].wait()
    moves = jnp.concatenate([move_ref[j] for j in range(slots)], axis=0)
    shape = (slots, templs)
    index = lax.broadcasted_iota(jnp.int32, shape, 0) * templs + lax.broadcasted_iota(jnp.int32, shape, 1)
    words_ref[...] = jnp.zeros_like(words_ref)
    index = index - jnp.where(index < slots // 2 * templs, 0, slots // 2 * templs)
    words_ref[:slots, :templs] = index * BLOCKS + (moves >> 7)
    words_ref[words : words + slots, :templs] = LANES - (moves & (LANES - 1))

    def send_up(device, rank, slot, back, twin):
        @pl.when(rank > mine)
        def _():
            pl.semaphore_wait(go_sem.at[back], 1)
            copy_to(slot, device, twin).start()

    each_peer(send_up)

    left = offsets.index((regions - 1) % regions)
    right = offsets.index(1 % regions)
    far = sorted({b for b in (left, right) if b})
    for b in far:
        copy_to(b * group + place, {"sub": sub}, b).wait_recv()
    listed = lambda b: recv_ref[pl.ds(pl.multiple_of((b * group + place) * stride, 8) + chans * SPEC_ROWS, 1), :].astype(jnp.int32)

    def row_of(b, channel):
        row = lax.rem(channel, chans) * slots_n + b * group + channel // chans
        return jnp.where(channel < 0, -1, row)

    from_left = jnp.where(region > 0, row_of(left, listed(left)), -1)
    from_right = jnp.where(region < regions - 1, row_of(right, listed(right)), -1)
    target = jnp.where(
        lane < own, row_of(0, lane), jnp.where(lane < own + bmax, from_left, from_right)
    )
    row = lax.rem(lax.broadcasted_iota(jnp.int32, (3 * total, 1), 0), total)
    picked = row_of(0, ids)
    for e in range(own, own + 2 * bmax):
        picked = jnp.where(ids == e, target[:, e : e + 1], picked)
    second = jnp.maximum(picked, 0) * BLOCKS + (moves >> 7)
    words_ref[2 * words : 2 * words + slots, :templs] = second
    fetch = pltpu.make_async_copy(words_ref, table_ref, load_sem.at[0])
    fetch.start()
    chosen_ref[...] = lax.dot_general(
        hot_ref[...], one(row == target), ACROSS, preferred_element_type=F32
    ).astype(BF16)
    fetch.wait()
    loads[11].wait()
    loads[12].wait()

    others = rows_of(slots_n - 1 - len(far))
    pltpu.make_async_copy(others, others, recv_sem.at[0]).wait()

    table = jnp.concatenate(
        [
            jnp.concatenate(
                [
                    recv_ref[pl.ds(c * SPEC_ROWS + i, slots_n, stride=stride), :]
                    for i in range(SPEC_ROWS)
                ],
                axis=1,
            )
            for c in range(chans)
        ],
        axis=0,
    )
    high = table.astype(BF16)
    rest = table - high.astype(F32)
    middle, low = split(rest)
    parts_ref[...] = jnp.concatenate([high, middle, low], axis=0)
    spec = dot(chosen_ref[...], parts_ref[...])
    xr, xi = spec[:, :BAND], spec[:, BAND:]
    wr, wi = tspec_ref[:, :BAND], tspec_ref[:, BAND:]
    lhs_ref[:, :BAND] = (wr * xr + wi * xi).astype(BF16)
    lhs_ref[:, BAND:] = (wr * xi - wi * xr).astype(BF16)
    filtered = 2.0 / NF * dot(high, lag_ref[...])
    power = filtered * filtered
    block = lambda i: power[:, LANES * i : LANES * (i + 1)]
    pieces = jnp.concatenate(
        [
            jnp.concatenate([block(q), block(q + 1) + block(q + 2), block(q + 3), block(q + 4)], axis=1)
            for q in range(BLOCKS)
        ],
        axis=0,
    )
    step = 2 * LANES
    rows_out = OUT // LANES
    lanes = lax.broadcasted_iota(jnp.int32, (8, LANES), 1)
    half = slots // 2 * templs

    def correlate(part, c):
        rows = slice(half * part, wide if part else half)
        corr = dot(lhs_ref[rows, :], lag_ref[:, c : c + step])
        for k in range(step // LANES):
            line_refs[part][pl.ds(c // LANES + k, rows.stop - rows.start, stride=BLOCKS), :] = (
                corr[:, LANES * k : LANES * (k + 1)] * weight_ref[rows, :]
            )

    def align(part, t):
        whole = jnp.zeros((8, LANES), F32)
        near = jnp.zeros((8, LANES), F32)
        for j in range(slots // 2 * part, slots if part else slots // 2):
            at, turn, norm_at = (table_ref[words * i + j, t] for i in range(3))
            value = line_refs[part][pl.ds(at, 8), :] * norms_ref[pl.ds(norm_at, 8), :]
            value = pltpu.roll(value, turn, 1)
            whole += value
            near += jnp.where(lanes < turn, value, 0.0)
        rest = whole - near
        sums_ref[part, rows_out * t : rows_out * (t + 1), :] = near[:rows_out] + rest[1 : rows_out + 1]

    for c in range(0, LN, step):
        correlate(0, c)
        if c == 0:
            energy = dot(pieces.astype(BF16), window_ref[...])
            norm = lax.rsqrt(energy + EPSILON)
            for q in range(BLOCKS):
                norms_ref[pl.ds(q, total, stride=BLOCKS), :] = norm[total * q : total * (q + 1)]
    chunks = LN // step
    for c in range(chunks):
        correlate(1, c * step)
        for t in range(templs * c // chunks, templs * (c + 1) // chunks):
            align(0, t)
    for t in range(templs):
        align(1, t)
    for a in range(rows_out):
        at = pl.ds(a, templs, stride=rows_out)
        out_ref[:, LANES * a : LANES * (a + 1)] = sums_ref[0, at, :] + sums_ref[1, at, :]

    others = rows_of(slots_n - 1)
    pltpu.make_async_copy(others, others, send_sem).wait()


def on_device(geometry, waveforms, templates, channel_ids, moveouts, active, border, border_count):
    regions, tmpls, subs, offsets = geometry
    slots_n = tmpls * subs * len(offsets)
    chans = waveforms.shape[1]
    bmax = border.shape[2]
    templs, slots = channel_ids.shape[1:]
    wide, total = slots * templs, slots_n * chans
    by_slot = lambda x: jnp.transpose(x, (2, 0, 1))
    short_table, lag_table = wide_tables()
    gather, twiddle, steps, window = small_tables(chans)
    waves = waveforms[0].reshape(chans, RES, LANES).swapaxes(0, 1).reshape(RES * chans, LANES)
    rows = jnp.swapaxes(templates[0], 0, 1).reshape(wide, K)
    inputs = (
        waves, gather, twiddle, steps, border[0], border_count, rows, short_table,
        by_slot(channel_ids), active, by_slot(moveouts), window, lag_table,
    )
    spaces = [pltpu.VMEM] * len(inputs)
    words = 3 * (-(-slots // 8) * 8), -(-templs // LANES) * LANES
    stride = -(-(chans * SPEC_ROWS + 1) // 8) * 8
    vmem = pltpu.VMEM
    scores = pl.pallas_call(
        functools.partial(kernel, geometry, spaces, bmax),
        out_shape=pltpu.VMEM((templs, OUT), F32),
        in_specs=[pl.BlockSpec(memory_space=pltpu.HBM)] * len(inputs),
        out_specs=pl.BlockSpec(memory_space=pltpu.VMEM),
        scratch_shapes=[
            *[space(x.shape, x.dtype) for space, x in zip(spaces, inputs)],
            vmem((slots_n * stride, LANES), F32),
            vmem((wide, 2 * BAND), F32),
            vmem((wide, LANES), BF16),
            vmem((wide, LANES), F32),
            vmem((wide, 3 * total), BF16),
            vmem((3 * total, 2 * BAND), BF16),
            vmem((total * BLOCKS + 8, LANES), F32),
            vmem((wide, 2 * BAND), BF16),
            vmem((slots // 2 * templs * BLOCKS + 8, LANES), F32),
            vmem(((slots - slots // 2) * templs * BLOCKS + 8, LANES), F32),
            vmem((2, templs * (OUT // LANES), LANES), F32),
            vmem(words, jnp.int32),
            pltpu.SMEM(words, jnp.int32),
            pltpu.SemaphoreType.DMA((len(inputs),)),
            pltpu.SemaphoreType.DMA,
            pltpu.SemaphoreType.DMA((len(offsets),)),
            pltpu.SemaphoreType.REGULAR((slots_n,)),
        ],
        compiler_params=pltpu.CompilerParams(
            collective_id=0, has_side_effects=True
        ),
        name="detect",
    )(*inputs)
    return scores[None]


def solution(mesh):
    regions, tmpls, subs = (mesh.shape[a] for a in ("region", "tmpl", "sub"))
    offsets = tuple(dict.fromkeys((0, (regions - 1) % regions, 1 % regions)))
    geometry = (regions, tmpls, subs, offsets)
    in_specs = (
        P("region", ("tmpl", "sub"), "groups"),
        P("region", ("tmpl", "sub"), None, None),
        P("region", ("tmpl", "sub"), None),
        P("region", ("tmpl", "sub"), None),
        P("region", ("tmpl", "sub")),
        P("region", None, None),
        P("region", None),
    )
    return jax.shard_map(
        functools.partial(on_device, geometry),
        mesh=mesh,
        in_specs=in_specs,
        out_specs=P("region", ("tmpl", "sub"), "groups"),
        check_vma=False,
    )
```

```python
import functools

import jax
import jax.numpy as jnp
import ml_dtypes
import numpy as np
from jax import lax
from jax.experimental import pallas as pl
from jax.experimental.pallas import tpu as pltpu
from jax.sharding import PartitionSpec as P

NF = 2048
F0 = 40
BAND = 384
K = 400
OUT = 512
LN = 1024
EPSILON = 1e-06

LANES = 128
RES = NF // LANES
STEPS = BAND // RES
COPIES = LANES // RES
PART = STEPS // COPIES
SPEC_ROWS = 2 * PART
BLOCKS = LN // LANES
SPAN = LN + OUT
MESH = pl.DeviceIdType.MESH
TURN = 2.0 * np.pi / NF
BF16, F32 = jnp.bfloat16, jnp.float32
ACROSS = (((1,), (1,)), ((), ()))


def as_bf16(x):
    return x.astype(np.float32).astype(ml_dtypes.bfloat16)


def halves(x):
    x = x.astype(np.float32)
    high = x.astype(ml_dtypes.bfloat16)
    return high, (x - high.astype(np.float32)).astype(ml_dtypes.bfloat16)


def bin_order():
    i, k, r = np.meshgrid(np.arange(PART), np.arange(COPIES), np.arange(RES), indexing="ij")
    return (F0 + RES * (PART * k + i) + r).reshape(-1)


def wide_tables():
    bins = bin_order()
    short = (np.arange(K)[:, None] * bins[None, :] % NF) * TURN
    short = np.concatenate([np.cos(short), -np.sin(short)], axis=1)
    lag = (bins[:, None] * np.arange(SPAN)[None, :] % NF) * TURN
    lag = np.concatenate([np.cos(lag), -np.sin(lag)], axis=0)
    return as_bf16(short), as_bf16(lag)


def small_tables(chans):
    r, a, b = np.arange(RES), np.arange(RES), np.arange(LANES)
    alpha = (F0 + r)[:, None] * a[None, :] * LANES % NF * TURN
    spread = lambda x: np.einsum("ra,cd->crad", x, np.eye(chans)).reshape(chans * RES, RES * chans)
    high, low = halves(np.concatenate([spread(np.cos(alpha)), spread(-np.sin(alpha))], axis=0))
    gather = np.concatenate([high, high, low], axis=1)
    theta = np.tile((F0 + r)[:, None] * b[None, :] % NF * TURN, (chans, 1))
    twiddle = np.concatenate([np.cos(theta), np.sin(theta)], axis=0).astype(np.float32)
    rows = np.zeros((COPIES, 8, 2 * LANES))
    for k in range(COPIES):
        beta = (PART * k + np.arange(PART))[:, None] * b[None, :] * RES % NF * TURN
        rows[k, :PART] = np.concatenate([np.cos(beta), np.sin(beta)], axis=1)
        rows[k, PART : 2 * PART] = np.concatenate([-np.sin(beta), np.cos(beta)], axis=1)
    steps = np.concatenate(halves(rows.reshape(8 * COPIES, 2 * LANES)), axis=0)
    window = []
    for i in (0, 1, 3, 4):
        place = LANES * i + b[:, None] - b[None, :]
        window.append((place >= 0) & (place < K))
    return gather, twiddle, steps, as_bf16(np.concatenate(window, axis=0))


def split(x):
    high = x.astype(BF16)
    return high, (x - high.astype(F32)).astype(BF16)


def dot(a, b):
    return jnp.dot(a, b, preferred_element_type=F32)


def kernel(geometry, spaces, bmax, *refs):
    count = len(spaces)
    hbm, out_ref, local = refs[:count], refs[count], refs[count + 1 : 2 * count + 1]
    (
        recv_ref, tspec_ref, hot_ref, moves_ref, weight_ref, chosen_ref, parts_ref, norms_ref,
        lhs_ref, corr_ref, load_sem, send_sem, recv_sem, go_sem,
    ) = refs[2 * count + 1 :]
    loads = [pltpu.make_async_copy(h, v, load_sem.at[i]) for i, (h, v) in enumerate(zip(hbm, local))]
    for load in loads:
        load.start()
    (
        wave_ref, gather_ref, twiddle_ref, steps_ref, border_ref, count_ref, tmpl_ref, short_ref,
        ids_ref, active_ref, move_ref, window_ref, lag_ref,
    ) = local
    regions, tmpls, subs, offsets = geometry
    group, blocks = tmpls * subs, len(offsets)
    slots_n = group * blocks
    region, tmpl, sub = (lax.axis_index(a) for a in ("region", "tmpl", "sub"))
    place = tmpl * subs + sub

    def rank_of(far, there, other):
        along = (there - 1) * (1 - far % 2) + (tmpls - 1 - there) * (far % 2)
        late = regions + far * (tmpls - 1) + along
        return jnp.where(there == 0, far, late) * subs + other

    mine = rank_of(region, tmpl, sub)
    chans = wave_ref.shape[0] // RES
    pay_rows = chans * SPEC_ROWS + 1
    stride = -(-pay_rows // 8) * 8
    own = group * chans
    total = slots_n * chans
    slots, _, templs = ids_ref.shape
    wide = slots * templs

    def peer(index):
        there, other = index // (blocks * subs), index % subs
        block = index // subs % blocks
        if regions == blocks:
            far = block
            step = lax.rem(region - far + regions, regions)
            block = jnp.where(step == 0, 0, jnp.where(step == regions - 1, 1, 2))
        else:
            step = (0, regions - 1, 1)[block]
            far = lax.rem(region + regions - step, regions)
        back = lax.rem(regions - step, regions)
        back = jnp.where(back == 0, 0, jnp.where(back == regions - 1, 1, 2))
        device = {"region": far, "tmpl": there, "sub": other}
        rank = rank_of(far, there, other)
        twin = jnp.where((there == tmpl) & (other == sub), block, 0)
        return device, rank, block * group + place, back * group + there * subs + other, twin

    def each_peer(action):
        for i in range(slots_n):
            action(*peer(i))

    def slot_rows(slot):
        return recv_ref.at[pl.ds(pl.multiple_of(slot * stride, 8), pay_rows), :]

    def copy_to(slot, device, lane):
        return pltpu.make_async_remote_copy(
            src_ref=slot_rows(place), dst_ref=slot_rows(slot), send_sem=send_sem,
            recv_sem=recv_sem.at[lane], device_id=device, device_id_type=MESH,
        )

    def rows_of(copies):
        return recv_ref.at[pl.ds(0, copies * pay_rows), :]

    barrier = pltpu.get_barrier_semaphore()
    lower = jnp.int32(0)
    for i in range(slots_n):
        device, rank = peer(i)[:2]

        @pl.when(rank > mine)
        def _():
            pl.semaphore_signal(barrier, inc=1, device_id=device, device_id_type=MESH)

        lower += jnp.where(rank < mine, 1, 0)

    start = pl.multiple_of(place * stride, 8)
    loads[4].wait()
    loads[5].wait()
    lane = lax.broadcasted_iota(jnp.int32, (1, LANES), 1)
    info = start + chans * SPEC_ROWS
    recv_ref[pl.ds(info, 1), :] = jnp.full((1, LANES), -1.0, F32)
    for i, side in enumerate((1, 0)):
        live = lane[:, :bmax] < count_ref[:, side : side + 1]
        listed = jnp.where(live, border_ref[side : side + 1, :], -1).astype(F32)
        recv_ref[pl.ds(info, 1), own + i * bmax : own + (i + 1) * bmax] = listed

    loads[0].wait()
    loads[1].wait()
    high, low = split(wave_ref[...])
    y = dot(gather_ref[...], jnp.concatenate([high, low, high], axis=0))
    half = RES * chans
    loads[2].wait()
    cos, sin = twiddle_ref[:half, :], twiddle_ref[half:, :]
    yr, yi = y[:half], y[half:]
    z = jnp.concatenate([yr * cos + yi * sin, yi * cos - yr * sin], axis=1)
    repeat = lambda x: jnp.concatenate(
        [x[RES * c : RES * (c + 1)] for c in range(chans) for _ in range(COPIES)], axis=0
    )
    high, low = split(z)
    loads[3].wait()
    nt = lambda a, b: lax.dot_general(a, b, ACROSS, preferred_element_type=F32)
    first = nt(steps_ref[...], repeat(high))
    x = first[: 8 * COPIES] + (first[8 * COPIES :] + nt(steps_ref[: 8 * COPIES, :], repeat(low)))
    for c in range(chans):
        piece = x[:8, LANES * c : LANES * (c + 1)]
        for k in range(1, COPIES):
            piece = jnp.where(
                lane >= RES * k, x[8 * k : 8 * (k + 1), LANES * c : LANES * (c + 1)], piece
            )
        recv_ref[pl.ds(start + c * SPEC_ROWS, SPEC_ROWS), :] = piece[:SPEC_ROWS]

    @pl.when(lower > 0)
    def _():
        pl.semaphore_wait(barrier, lower)

    def send_down(device, rank, slot, back, twin):
        @pl.when(rank < mine)
        def _():
            copy_to(slot, device, twin).start()

    each_peer(send_down)

    def announce(device, rank, slot, back, twin):
        @pl.when(rank < mine)
        def _():
            pl.semaphore_signal(go_sem.at[slot], inc=1, device_id=device, device_id_type=MESH)

    each_peer(announce)

    loads[6].wait()
    loads[7].wait()
    waves = tmpl_ref[...]
    tspec_ref[...] = dot(waves, short_ref[...])
    waves = waves.astype(F32)
    power = jnp.sum(waves * waves, axis=1, keepdims=True)
    loads[8].wait()
    loads[9].wait()
    square = (templs, templs)
    same = lax.broadcasted_iota(jnp.int32, square, 0) == lax.broadcasted_iota(jnp.int32, square, 1)
    column = lambda x: jnp.sum(jnp.where(same, x, 0), axis=1, keepdims=True, dtype=jnp.int32)
    used = column(active_ref[...])
    id_rows = jnp.concatenate([column(ids_ref[j]) for j in range(slots)], axis=0)
    live = jnp.concatenate([jnp.where(used > j, 1.0, 0.0) for j in range(slots)], axis=0)
    one = lambda mask: jnp.where(mask, 1.0, 0.0).astype(BF16)
    hot_ref[...] = one(id_rows == lane)
    scale = 2.0 / NF * lax.rsqrt(power + EPSILON) * live
    scale_high = scale.astype(BF16).astype(F32)
    part = lax.broadcasted_iota(jnp.int32, (1, 3 * total), 1)
    weight_ref[...] = jnp.where(part < 2 * total, scale_high, scale - scale_high).astype(BF16)
    loads[10].wait()
    moves = jnp.concatenate([column(move_ref[j]) for j in range(slots)], axis=0)
    moves_ref[...] = jnp.broadcast_to(moves, (wide, LANES))

    def send_up(device, rank, slot, back, twin):
        @pl.when(rank > mine)
        def _():
            pl.semaphore_wait(go_sem.at[back], 1)
            copy_to(slot, device, twin).start()

    each_peer(send_up)

    left = offsets.index((regions - 1) % regions)
    right = offsets.index(1 % regions)
    far = sorted({b for b in (left, right) if b})
    for b in far:
        copy_to(b * group + place, {"sub": sub}, b).wait_recv()
    listed = lambda b: recv_ref[pl.ds(pl.multiple_of((b * group + place) * stride, 8) + chans * SPEC_ROWS, 1), :].astype(jnp.int32)

    def row_of(b, channel):
        row = lax.rem(channel, chans) * slots_n + b * group + channel // chans
        return jnp.where(channel < 0, -1, row)

    from_left = jnp.where(region > 0, row_of(left, listed(left)), -1)
    from_right = jnp.where(region < regions - 1, row_of(right, listed(right)), -1)
    target = jnp.where(
        lane < own, row_of(0, lane), jnp.where(lane < own + bmax, from_left, from_right)
    )
    row = lax.rem(lax.broadcasted_iota(jnp.int32, (3 * total, 1), 0), total)
    chosen = lax.dot_general(hot_ref[...], one(row == target), ACROSS, preferred_element_type=F32)
    chosen_ref[...] = chosen.astype(BF16)
    weight_ref[...] = (chosen * weight_ref[...].astype(F32)).astype(BF16)
    loads[11].wait()
    loads[12].wait()

    others = rows_of(slots_n - 1 - len(far))
    pltpu.make_async_copy(others, others, recv_sem.at[0]).wait()

    table = jnp.concatenate(
        [
            jnp.concatenate(
                [
                    recv_ref[pl.ds(c * SPEC_ROWS + i, slots_n, stride=stride), :]
                    for i in range(SPEC_ROWS)
                ],
                axis=1,
            )
            for c in range(chans)
        ],
        axis=0,
    )
    high = table.astype(BF16)
    rest = table - high.astype(F32)
    middle, low = split(rest)
    parts_ref[...] = jnp.concatenate([high, middle, low], axis=0)
    lhs_ref[:total, :] = high
    spec = dot(chosen_ref[...], parts_ref[...])
    late = dot(high, lag_ref[:, LN:])
    xr, xi = spec[:, :BAND], spec[:, BAND:]
    wr, wi = tspec_ref[:, :BAND], tspec_ref[:, BAND:]
    lhs_ref[total:, :BAND] = (wr * xr + wi * xi).astype(BF16)
    lhs_ref[total:, BAND:] = (wr * xi - wi * xr).astype(BF16)
    step = 2 * LANES
    half = slots // 2 * templs
    parts = (slice(0, half), slice(half, wide))
    filtered = []
    for c in range(0, LN, step):
        corr = dot(lhs_ref[: total + half, :], lag_ref[:, c : c + step])
        filtered.append(corr[:total])
        corr_ref[parts[0], c : c + step] = corr[total:]
    filtered = 2.0 / NF * jnp.concatenate([*filtered, late], axis=1)
    power = filtered * filtered
    block = lambda i: power[:, LANES * i : LANES * (i + 1)]
    pieces = jnp.concatenate(
        [
            jnp.concatenate([block(q), block(q + 1) + block(q + 2), block(q + 3), block(q + 4)], axis=1)
            for q in range(BLOCKS)
        ],
        axis=0,
    )

    def correlate(c):
        corr_ref[parts[1], c : c + step] = dot(lhs_ref[total + half :, :], lag_ref[:, c : c + step])

    correlate(0)
    energy = dot(pieces.astype(BF16), window_ref[...])
    for c in range(step, LN, step):
        correlate(c)
    high, middle = split(lax.rsqrt(energy + EPSILON))
    for q in range(BLOCKS):
        at, rows = slice(LANES * q, LANES * (q + 1)), slice(total * q, total * (q + 1))
        norms_ref[:total, at] = high[rows]
        norms_ref[total : 2 * total, at] = middle[rows]
        norms_ref[2 * total :, at] = high[rows]

    rows_out = OUT // LANES
    lanes = lax.broadcasted_iota(jnp.int32, (8, LANES), 1)
    scores = [[jnp.zeros((8, LANES), F32)] * rows_out for _ in range(templs // 8)]

    def normalise(part, c):
        at = slice(c, c + step)
        corr_ref[parts[part], at] *= dot(weight_ref[parts[part], :], norms_ref[:, at])

    def align(j, g):
        rows = slice(j * templs + 8 * g, j * templs + 8 * g + 8)
        move = moves_ref[rows, :]
        odd, far_pair, turn = (move & LANES) != 0, (move & (2 * LANES)) != 0, move & (LANES - 1)
        value = [corr_ref[rows, LANES * i : LANES * (i + 1)] for i in range(BLOCKS)]
        value = [jnp.where(odd, value[i + 1], value[i]) for i in range(BLOCKS - 1)]
        value = [jnp.where(far_pair, value[i + 2], value[i]) for i in range(rows_out + 1)]
        index, near = (lanes + turn) & (LANES - 1), lanes < LANES - turn
        value = [jnp.take_along_axis(x, index, axis=1) for x in value]
        for i in range(rows_out):
            scores[g][i] = scores[g][i] + jnp.where(near, value[i], value[i + 1])

    for part in range(2):
        for c in range(0, LN, step):
            normalise(part, c)
        for g in range(templs // 8):
            for j in range(slots // 2 * part, slots if part else slots // 2):
                align(j, g)
    for g in range(templs // 8):
        for i in range(rows_out):
            out_ref[8 * g : 8 * g + 8, LANES * i : LANES * (i + 1)] = scores[g][i]

    others = rows_of(slots_n - 1)
    pltpu.make_async_copy(others, others, send_sem).wait()


def on_device(geometry, waveforms, templates, channel_ids, moveouts, active, border, border_count):
    regions, tmpls, subs, offsets = geometry
    slots_n = tmpls * subs * len(offsets)
    chans = waveforms.shape[1]
    bmax = border.shape[2]
    templs, slots = channel_ids.shape[1:]
    wide, total = slots * templs, slots_n * chans
    by_slot = lambda x: jnp.transpose(x, (2, 0, 1))
    short_table, lag_table = wide_tables()
    gather, twiddle, steps, window = small_tables(chans)
    waves = waveforms[0].reshape(chans, RES, LANES).swapaxes(0, 1).reshape(RES * chans, LANES)
    rows = jnp.swapaxes(templates[0], 0, 1).reshape(wide, K)
    inputs = (
        waves, gather, twiddle, steps, border[0], border_count, rows, short_table,
        by_slot(channel_ids), active, by_slot(moveouts), window, lag_table,
    )
    spaces = [pltpu.VMEM] * len(inputs)
    stride = -(-(chans * SPEC_ROWS + 1) // 8) * 8
    vmem = pltpu.VMEM
    scores = pl.pallas_call(
        functools.partial(kernel, geometry, spaces, bmax),
        out_shape=pltpu.VMEM((templs, OUT), F32),
        in_specs=[pl.BlockSpec(memory_space=pltpu.HBM)] * len(inputs),
        out_specs=pl.BlockSpec(memory_space=pltpu.VMEM),
        scratch_shapes=[
            *[space(x.shape, x.dtype) for space, x in zip(spaces, inputs)],
            vmem((slots_n * stride, LANES), F32),
            vmem((wide, 2 * BAND), F32),
            vmem((wide, LANES), BF16),
            vmem((wide, LANES), jnp.int32),
            vmem((wide, 3 * total), BF16),
            vmem((wide, 3 * total), BF16),
            vmem((3 * total, 2 * BAND), BF16),
            vmem((3 * total, LN), BF16),
            vmem((total + wide, 2 * BAND), BF16),
            vmem((wide, LN), F32),
            pltpu.SemaphoreType.DMA((len(inputs),)),
            pltpu.SemaphoreType.DMA,
            pltpu.SemaphoreType.DMA((len(offsets),)),
            pltpu.SemaphoreType.REGULAR((slots_n,)),
        ],
        compiler_params=pltpu.CompilerParams(
            collective_id=0, has_side_effects=True
        ),
        name="detect",
    )(*inputs)
    return scores[None]


def solution(mesh):
    regions, tmpls, subs = (mesh.shape[a] for a in ("region", "tmpl", "sub"))
    offsets = tuple(dict.fromkeys((0, (regions - 1) % regions, 1 % regions)))
    geometry = (regions, tmpls, subs, offsets)
    in_specs = (
        P("region", ("tmpl", "sub"), "groups"),
        P("region", ("tmpl", "sub"), None, None),
        P("region", ("tmpl", "sub"), None),
        P("region", ("tmpl", "sub"), None),
        P("region", ("tmpl", "sub")),
        P("region", None, None),
        P("region", None),
    )
    return jax.shard_map(
        functools.partial(on_device, geometry),
        mesh=mesh,
        in_specs=in_specs,
        out_specs=P("region", ("tmpl", "sub"), "groups"),
        check_vma=False,
    )
```

```python
import functools

import jax
import jax.numpy as jnp
import ml_dtypes
import numpy as np
from jax import lax
from jax.experimental import pallas as pl
from jax.experimental.pallas import tpu as pltpu
from jax.sharding import PartitionSpec as P

NF = 2048
F0 = 40
BAND = 384
K = 400
OUT = 512
LN = 1024
EPSILON = 1e-06

LANES = 128
RES = NF // LANES
STEPS = BAND // RES
COPIES = LANES // RES
PART = STEPS // COPIES
SPEC_ROWS = 2 * PART
BLOCKS = LN // LANES
SPAN = LN + OUT
SHIFTS = BLOCKS - OUT // LANES
MESH = pl.DeviceIdType.MESH
TURN = 2.0 * np.pi / NF
BF16, F32 = jnp.bfloat16, jnp.float32
ACROSS = (((1,), (1,)), ((), ()))


def as_bf16(x):
    return x.astype(np.float32).astype(ml_dtypes.bfloat16)


def halves(x):
    x = x.astype(np.float32)
    high = x.astype(ml_dtypes.bfloat16)
    return high, (x - high.astype(np.float32)).astype(ml_dtypes.bfloat16)


def bin_order():
    i, k, r = np.meshgrid(np.arange(PART), np.arange(COPIES), np.arange(RES), indexing="ij")
    return (F0 + RES * (PART * k + i) + r).reshape(-1)


def wide_tables():
    bins = bin_order()
    short = (np.arange(K)[:, None] * bins[None, :] % NF) * TURN
    short = np.concatenate([np.cos(short), -np.sin(short)], axis=1)
    lag = (bins[:, None] * np.arange(SPAN)[None, :] % NF) * TURN
    lag = np.concatenate([np.cos(lag), -np.sin(lag)], axis=0)
    return as_bf16(short), as_bf16(lag)


def small_tables(chans):
    r, a, b = np.arange(RES), np.arange(RES), np.arange(LANES)
    alpha = (F0 + r)[:, None] * a[None, :] * LANES % NF * TURN
    spread = lambda x: np.einsum("ra,cd->crad", x, np.eye(chans)).reshape(chans * RES, RES * chans)
    high, low = halves(np.concatenate([spread(np.cos(alpha)), spread(-np.sin(alpha))], axis=0))
    gather = np.concatenate([high, high, low], axis=1)
    theta = np.tile((F0 + r)[:, None] * b[None, :] % NF * TURN, (chans, 1))
    twiddle = np.concatenate([np.cos(theta), np.sin(theta)], axis=0).astype(np.float32)
    rows = np.zeros((COPIES, 8, 2 * LANES))
    for k in range(COPIES):
        beta = (PART * k + np.arange(PART))[:, None] * b[None, :] * RES % NF * TURN
        rows[k, :PART] = np.concatenate([np.cos(beta), np.sin(beta)], axis=1)
        rows[k, PART : 2 * PART] = np.concatenate([-np.sin(beta), np.cos(beta)], axis=1)
    steps = np.concatenate(halves(rows.reshape(8 * COPIES, 2 * LANES)), axis=0)
    window = []
    for i in (0, 1, 3, 4):
        place = LANES * i + b[:, None] - b[None, :]
        window.append((place >= 0) & (place < K))
    return gather, twiddle, steps, as_bf16(np.concatenate(window, axis=0))


def split(x):
    high = x.astype(BF16)
    return high, (x - high.astype(F32)).astype(BF16)


def dot(a, b):
    return jnp.dot(a, b, preferred_element_type=F32)


def kernel(geometry, spaces, bmax, *refs):
    count = len(spaces)
    hbm, out_ref, local = refs[:count], refs[count], refs[count + 1 : 2 * count + 1]
    (
        recv_ref, tspec_ref, hot_ref, moves_ref, weight_ref, chosen_ref, parts_ref, norms_ref,
        lhs_ref, corr_ref, near_ref, scale_ref, load_sem, send_sem, recv_sem, go_sem,
    ) = refs[2 * count + 1 :]
    loads = [pltpu.make_async_copy(h, v, load_sem.at[i]) for i, (h, v) in enumerate(zip(hbm, local))]
    for load in loads:
        load.start()
    (
        wave_ref, gather_ref, twiddle_ref, steps_ref, border_ref, count_ref, tmpl_ref, short_ref,
        ids_ref, active_ref, move_ref, window_ref, lag_ref,
    ) = local
    regions, tmpls, subs, offsets = geometry
    group, blocks = tmpls * subs, len(offsets)
    slots_n = group * blocks
    region, tmpl, sub = (lax.axis_index(a) for a in ("region", "tmpl", "sub"))
    place = tmpl * subs + sub

    def rank_of(far, there, other):
        along = (there - 1) * (1 - far % 2) + (tmpls - 1 - there) * (far % 2)
        late = regions + far * (tmpls - 1) + along
        return jnp.where(there == 0, far, late) * subs + other

    mine = rank_of(region, tmpl, sub)
    chans = wave_ref.shape[0] // RES
    pay_rows = chans * SPEC_ROWS + 1
    stride = -(-pay_rows // 8) * 8
    own = group * chans
    total = slots_n * chans
    slots, _, templs = ids_ref.shape
    wide = slots * templs

    def peer(index):
        there, other = index // (blocks * subs), index % subs
        block = index // subs % blocks
        if regions == blocks:
            far = block
            step = lax.rem(region - far + regions, regions)
            block = jnp.where(step == 0, 0, jnp.where(step == regions - 1, 1, 2))
        else:
            step = (0, regions - 1, 1)[block]
            far = lax.rem(region + regions - step, regions)
        back = lax.rem(regions - step, regions)
        back = jnp.where(back == 0, 0, jnp.where(back == regions - 1, 1, 2))
        device = {"region": far, "tmpl": there, "sub": other}
        rank = rank_of(far, there, other)
        twin = jnp.where((there == tmpl) & (other == sub), block, 0)
        return device, rank, block * group + place, back * group + there * subs + other, twin

    def each_peer(action):
        for i in range(slots_n):
            action(*peer(i))

    def slot_rows(slot):
        return recv_ref.at[pl.ds(pl.multiple_of(slot * stride, 8), pay_rows), :]

    def copy_to(slot, device, lane):
        return pltpu.make_async_remote_copy(
            src_ref=slot_rows(place), dst_ref=slot_rows(slot), send_sem=send_sem,
            recv_sem=recv_sem.at[lane], device_id=device, device_id_type=MESH,
        )

    def rows_of(copies):
        return recv_ref.at[pl.ds(0, copies * pay_rows), :]

    barrier = pltpu.get_barrier_semaphore()
    lower = jnp.int32(0)
    for i in range(slots_n):
        device, rank = peer(i)[:2]

        @pl.when(rank > mine)
        def _():
            pl.semaphore_signal(barrier, inc=1, device_id=device, device_id_type=MESH)

        lower += jnp.where(rank < mine, 1, 0)

    start = pl.multiple_of(place * stride, 8)
    lane = lax.broadcasted_iota(jnp.int32, (1, LANES), 1)
    loads[0].wait()
    loads[1].wait()
    high, low = split(wave_ref[...])
    y = dot(gather_ref[...], jnp.concatenate([high, low, high], axis=0))
    half = RES * chans
    loads[2].wait()
    cos, sin = twiddle_ref[:half, :], twiddle_ref[half:, :]
    yr, yi = y[:half], y[half:]
    z = jnp.concatenate([yr * cos + yi * sin, yi * cos - yr * sin], axis=1)
    repeat = lambda x: jnp.concatenate(
        [x[RES * c : RES * (c + 1)] for c in range(chans) for _ in range(COPIES)], axis=0
    )
    high, low = split(z)
    loads[3].wait()
    nt = lambda a, b: lax.dot_general(a, b, ACROSS, preferred_element_type=F32)
    first = nt(steps_ref[...], repeat(high))
    x = first[: 8 * COPIES] + (first[8 * COPIES :] + nt(steps_ref[: 8 * COPIES, :], repeat(low)))
    loads[4].wait()
    loads[5].wait()
    info = start + chans * SPEC_ROWS
    recv_ref[pl.ds(info, 1), :] = jnp.full((1, LANES), -1.0, F32)
    for i, side in enumerate((1, 0)):
        live = lane[:, :bmax] < count_ref[:, side : side + 1]
        listed = jnp.where(live, border_ref[side : side + 1, :], -1).astype(F32)
        recv_ref[pl.ds(info, 1), own + i * bmax : own + (i + 1) * bmax] = listed
    for c in range(chans):
        piece = x[:8, LANES * c : LANES * (c + 1)]
        for k in range(1, COPIES):
            piece = jnp.where(
                lane >= RES * k, x[8 * k : 8 * (k + 1), LANES * c : LANES * (c + 1)], piece
            )
        recv_ref[pl.ds(start + c * SPEC_ROWS, SPEC_ROWS), :] = piece[:SPEC_ROWS]

    @pl.when(lower > 0)
    def _():
        pl.semaphore_wait(barrier, lower)

    def send_down(device, rank, slot, back, twin):
        @pl.when(rank < mine)
        def _():
            copy_to(slot, device, twin).start()

    each_peer(send_down)

    def announce(device, rank, slot, back, twin):
        @pl.when(rank < mine)
        def _():
            pl.semaphore_signal(go_sem.at[slot], inc=1, device_id=device, device_id_type=MESH)

    each_peer(announce)

    loads[6].wait()
    loads[7].wait()
    waves = tmpl_ref[...]
    tspec_ref[...] = dot(waves, short_ref[...])
    waves = waves.astype(F32)
    power = jnp.sum(waves * waves, axis=1, keepdims=True)
    loads[8].wait()
    loads[9].wait()
    square = (templs, templs)
    same = lax.broadcasted_iota(jnp.int32, square, 0) == lax.broadcasted_iota(jnp.int32, square, 1)
    column = lambda x: jnp.sum(jnp.where(same, x, 0), axis=1, keepdims=True, dtype=jnp.int32)
    used = column(active_ref[...])
    id_rows = jnp.concatenate([column(ids_ref[j]) for j in range(slots)], axis=0)
    live = jnp.concatenate([jnp.where(used > j, 1.0, 0.0) for j in range(slots)], axis=0)
    one = lambda mask: jnp.where(mask, 1.0, 0.0).astype(BF16)
    hot_ref[...] = one(id_rows == lane)
    scale = 2.0 / NF * lax.rsqrt(power + EPSILON) * live
    scale_ref[...] = jnp.broadcast_to(scale, (wide, LANES))
    loads[10].wait()
    moves = jnp.concatenate([column(move_ref[j]) for j in range(slots)], axis=0)
    moves_ref[...] = jnp.broadcast_to(moves, (wide, LANES))

    def send_up(device, rank, slot, back, twin):
        @pl.when(rank > mine)
        def _():
            pl.semaphore_wait(go_sem.at[back], 1)
            copy_to(slot, device, twin).start()

    each_peer(send_up)

    left = offsets.index((regions - 1) % regions)
    right = offsets.index(1 % regions)
    far = sorted({b for b in (left, right) if b})
    for b in far:
        copy_to(b * group + place, {"sub": sub}, b).wait_recv()
    listed = lambda b: recv_ref[pl.ds(pl.multiple_of((b * group + place) * stride, 8) + chans * SPEC_ROWS, 1), :].astype(jnp.int32)

    def row_of(b, channel):
        row = lax.rem(channel, chans) * slots_n + b * group + channel // chans
        return jnp.where(channel < 0, -1, row)

    from_left = jnp.where(region > 0, row_of(left, listed(left)), -1)
    from_right = jnp.where(region < regions - 1, row_of(right, listed(right)), -1)
    target = jnp.where(
        lane < own, row_of(0, lane), jnp.where(lane < own + bmax, from_left, from_right)
    )
    row = lax.rem(lax.broadcasted_iota(jnp.int32, (2 * SHIFTS * total, 1), 0), total)
    chosen = lax.dot_general(hot_ref[...], one(row == target), ACROSS, preferred_element_type=F32)
    chosen_ref[...] = chosen[:, : 3 * total].astype(BF16)
    shift = lax.rem(lax.broadcasted_iota(jnp.int32, (1, 2 * SHIFTS * total), 1) // total, SHIFTS)
    weight_ref[...] = jnp.where(shift == moves_ref[:, :1] // LANES, chosen, 0.0).astype(BF16)
    loads[11].wait()
    loads[12].wait()

    others = rows_of(slots_n - 1 - len(far))
    pltpu.make_async_copy(others, others, recv_sem.at[0]).wait()

    table = jnp.concatenate(
        [
            jnp.concatenate(
                [
                    recv_ref[pl.ds(c * SPEC_ROWS + i, slots_n, stride=stride), :]
                    for i in range(SPEC_ROWS)
                ],
                axis=1,
            )
            for c in range(chans)
        ],
        axis=0,
    )
    high = table.astype(BF16)
    rest = table - high.astype(F32)
    middle, low = split(rest)
    parts_ref[...] = jnp.concatenate([high, middle, low], axis=0)
    lhs_ref[:total, :] = high
    spec = dot(chosen_ref[...], parts_ref[...])
    late = dot(high, lag_ref[:, LN:])
    xr, xi = spec[:, :BAND], spec[:, BAND:]
    wr, wi = tspec_ref[:, :BAND], tspec_ref[:, BAND:]
    lhs_ref[total:, :BAND] = (wr * xr + wi * xi).astype(BF16)
    lhs_ref[total:, BAND:] = (wr * xi - wi * xr).astype(BF16)
    step = 4 * LANES
    half = slots // 2 * templs
    parts = (slice(0, half), slice(half, wide))
    filtered = []
    for c in range(0, LN, step):
        corr = dot(lhs_ref[: total + half, :], lag_ref[:, c : c + step])
        filtered.append(corr[:total])
        corr_ref[parts[0], c : c + step] = corr[total:]
    filtered = 2.0 / NF * jnp.concatenate([*filtered, late], axis=1)
    power = filtered * filtered
    block = lambda i: power[:, LANES * i : LANES * (i + 1)]
    pieces = jnp.concatenate(
        [
            jnp.concatenate([block(q), block(q + 1) + block(q + 2), block(q + 3), block(q + 4)], axis=1)
            for q in range(BLOCKS)
        ],
        axis=0,
    )

    def correlate(c):
        corr_ref[parts[1], c : c + step] = dot(lhs_ref[total + half :, :], lag_ref[:, c : c + step])

    correlate(0)
    energy = dot(pieces.astype(BF16), window_ref[...])
    for c in range(step, LN, step):
        correlate(c)
    high, middle = split(lax.rsqrt(energy + EPSILON))
    span = SHIFTS * total
    for a in range(OUT // LANES + 1):
        at, rows = slice(LANES * a, LANES * (a + 1)), slice(total * a, total * a + span)
        norms_ref[:span, at] = high[rows]
        norms_ref[span:, at] = middle[rows]

    rows_out = OUT // LANES
    lanes = lax.broadcasted_iota(jnp.int32, (8, LANES), 1)
    scores = [[jnp.zeros((8, LANES), F32)] * rows_out for _ in range(templs // 8)]

    def gather_norms(part):
        near_ref[parts[part], :] = dot(weight_ref[parts[part], :], norms_ref[...])

    def align(j, g):
        rows = slice(j * templs + 8 * g, j * templs + 8 * g + 8)
        move = moves_ref[rows, :]
        odd, far_pair, turn = (move & LANES) != 0, (move & (2 * LANES)) != 0, move & (LANES - 1)
        value = [corr_ref[rows, LANES * i : LANES * (i + 1)] for i in range(BLOCKS)]
        value = [jnp.where(odd, value[i + 1], value[i]) for i in range(BLOCKS - 1)]
        value = [jnp.where(far_pair, value[i + 2], value[i]) for i in range(rows_out + 1)]
        index, near = (lanes + turn) & (LANES - 1), lanes < LANES - turn
        value = [
            jnp.take_along_axis(x * near_ref[rows, LANES * i : LANES * (i + 1)], index, axis=1)
            for i, x in enumerate(value)
        ]
        scale = scale_ref[rows, :]
        for i in range(rows_out):
            scores[g][i] = scores[g][i] + jnp.where(near, value[i], value[i + 1]) * scale

    for part in range(2):
        gather_norms(part)
        for g in range(templs // 8):
            for j in range(slots // 2 * part, slots if part else slots // 2):
                align(j, g)
    for g in range(templs // 8):
        for i in range(rows_out):
            out_ref[8 * g : 8 * g + 8, LANES * i : LANES * (i + 1)] = scores[g][i]

    others = rows_of(slots_n - 1)
    pltpu.make_async_copy(others, others, send_sem).wait()


def on_device(geometry, waveforms, templates, channel_ids, moveouts, active, border, border_count):
    regions, tmpls, subs, offsets = geometry
    slots_n = tmpls * subs * len(offsets)
    chans = waveforms.shape[1]
    bmax = border.shape[2]
    templs, slots = channel_ids.shape[1:]
    wide, total = slots * templs, slots_n * chans
    by_slot = lambda x: jnp.transpose(x, (2, 0, 1))
    short_table, lag_table = wide_tables()
    gather, twiddle, steps, window = small_tables(chans)
    waves = waveforms[0].reshape(chans, RES, LANES).swapaxes(0, 1).reshape(RES * chans, LANES)
    rows = jnp.swapaxes(templates[0], 0, 1).reshape(wide, K)
    inputs = (
        waves, gather, twiddle, steps, border[0], border_count, rows, short_table,
        by_slot(channel_ids), active, by_slot(moveouts), window, lag_table,
    )
    spaces = [pltpu.VMEM] * len(inputs)
    stride = -(-(chans * SPEC_ROWS + 1) // 8) * 8
    vmem = pltpu.VMEM
    scores = pl.pallas_call(
        functools.partial(kernel, geometry, spaces, bmax),
        out_shape=pltpu.VMEM((templs, OUT), F32),
        in_specs=[pl.BlockSpec(memory_space=pltpu.HBM)] * len(inputs),
        out_specs=pl.BlockSpec(memory_space=pltpu.VMEM),
        scratch_shapes=[
            *[space(x.shape, x.dtype) for space, x in zip(spaces, inputs)],
            vmem((slots_n * stride, LANES), F32),
            vmem((wide, 2 * BAND), F32),
            vmem((wide, LANES), BF16),
            vmem((wide, LANES), jnp.int32),
            vmem((wide, 2 * SHIFTS * total), BF16),
            vmem((wide, 3 * total), BF16),
            vmem((3 * total, 2 * BAND), BF16),
            vmem((2 * SHIFTS * total, OUT + LANES), BF16),
            vmem((total + wide, 2 * BAND), BF16),
            vmem((wide, LN), F32),
            vmem((wide, OUT + LANES), F32),
            vmem((wide, LANES), F32),
            pltpu.SemaphoreType.DMA((len(inputs),)),
            pltpu.SemaphoreType.DMA,
            pltpu.SemaphoreType.DMA((len(offsets),)),
            pltpu.SemaphoreType.REGULAR((slots_n,)),
        ],
        compiler_params=pltpu.CompilerParams(
            collective_id=0, has_side_effects=True
        ),
        name="detect",
    )(*inputs)
    return scores[None]


def solution(mesh):
    regions, tmpls, subs = (mesh.shape[a] for a in ("region", "tmpl", "sub"))
    offsets = tuple(dict.fromkeys((0, (regions - 1) % regions, 1 % regions)))
    geometry = (regions, tmpls, subs, offsets)
    in_specs = (
        P("region", ("tmpl", "sub"), "groups"),
        P("region", ("tmpl", "sub"), None, None),
        P("region", ("tmpl", "sub"), None),
        P("region", ("tmpl", "sub"), None),
        P("region", ("tmpl", "sub")),
        P("region", None, None),
        P("region", None),
    )
    return jax.shard_map(
        functools.partial(on_device, geometry),
        mesh=mesh,
        in_specs=in_specs,
        out_specs=P("region", ("tmpl", "sub"), "groups"),
        check_vma=False,
    )
```

```python
import functools

import jax
import jax.numpy as jnp
import ml_dtypes
import numpy as np
from jax import lax
from jax.experimental import pallas as pl
from jax.experimental.pallas import tpu as pltpu
from jax.sharding import PartitionSpec as P

NF = 2048
F0 = 40
BAND = 384
K = 400
OUT = 512
LN = 1024
EPSILON = 1e-06

LANES = 128
RES = NF // LANES
STEPS = BAND // RES
COPIES = LANES // RES
PART = STEPS // COPIES
SPEC_ROWS = 2 * PART
BLOCKS = LN // LANES
SHIFTS = BLOCKS - OUT // LANES
MESH = pl.DeviceIdType.MESH
TURN = 2.0 * np.pi / NF
BF16, F32 = jnp.bfloat16, jnp.float32
ACROSS = (((1,), (1,)), ((), ()))


def as_bf16(x):
    return x.astype(np.float32).astype(ml_dtypes.bfloat16)


def halves(x):
    x = x.astype(np.float32)
    high = x.astype(ml_dtypes.bfloat16)
    return high, (x - high.astype(np.float32)).astype(ml_dtypes.bfloat16)


def bin_order():
    i, k, r = np.meshgrid(np.arange(PART), np.arange(COPIES), np.arange(RES), indexing="ij")
    return (F0 + RES * (PART * k + i) + r).reshape(-1)


def wide_tables():
    bins = bin_order()
    short = (np.arange(K)[:, None] * bins[None, :] % NF) * TURN
    short = np.concatenate([np.cos(short), -np.sin(short)], axis=1)
    lag = (bins[:, None] * np.arange(LN)[None, :] % NF) * TURN
    lag = np.concatenate([np.cos(lag), -np.sin(lag)], axis=0)
    return as_bf16(short), as_bf16(lag)


def small_tables(chans):
    r, a, b = np.arange(RES), np.arange(RES), np.arange(LANES)
    alpha = (F0 + r)[:, None] * a[None, :] * LANES % NF * TURN
    spread = lambda x: np.einsum("ra,cd->crad", x, np.eye(chans)).reshape(chans * RES, RES * chans)
    high, low = halves(np.concatenate([spread(np.cos(alpha)), spread(-np.sin(alpha))], axis=0))
    gather = np.concatenate([high, high, low], axis=1)
    theta = np.tile((F0 + r)[:, None] * b[None, :] % NF * TURN, (chans, 1))
    twiddle = np.concatenate([np.cos(theta), np.sin(theta)], axis=0).astype(np.float32)
    rows = np.zeros((COPIES, 8, 2 * LANES))
    for k in range(COPIES):
        beta = (PART * k + np.arange(PART))[:, None] * b[None, :] * RES % NF * TURN
        rows[k, :PART] = np.concatenate([np.cos(beta), np.sin(beta)], axis=1)
        rows[k, PART : 2 * PART] = np.concatenate([-np.sin(beta), np.cos(beta)], axis=1)
    steps = np.concatenate(halves(rows.reshape(8 * COPIES, 2 * LANES)), axis=0)
    window = []
    for i in (0, 1, 3, 4):
        place = LANES * i + b[:, None] - b[None, :]
        window.append((place >= 0) & (place < K))
    return gather, twiddle, steps, as_bf16(np.concatenate(window, axis=0))


def split(x):
    high = x.astype(BF16)
    return high, (x - high.astype(F32)).astype(BF16)


def dot(a, b):
    return jnp.dot(a, b, preferred_element_type=F32)


def kernel(geometry, spaces, bmax, *refs):
    count = len(spaces)
    hbm, out_ref, local = refs[:count], refs[count], refs[count + 1 : 2 * count + 1]
    (
        recv_ref, tspec_ref, hot_ref, moves_ref, weight_ref, chosen_ref, parts_ref, norms_ref,
        lhs_ref, corr_ref, near_ref, scale_ref, load_sem, send_sem, recv_sem, go_sem,
    ) = refs[2 * count + 1 :]
    loads = [pltpu.make_async_copy(h, v, load_sem.at[i]) for i, (h, v) in enumerate(zip(hbm, local))]
    for load in loads:
        load.start()
    (
        wave_ref, gather_ref, twiddle_ref, steps_ref, border_ref, count_ref, tmpl_ref, short_ref,
        ids_ref, active_ref, move_ref, window_ref, lag_ref,
    ) = local
    regions, tmpls, subs, offsets = geometry
    group, blocks = tmpls * subs, len(offsets)
    slots_n = group * blocks
    region, tmpl, sub = (lax.axis_index(a) for a in ("region", "tmpl", "sub"))
    place = tmpl * subs + sub

    def rank_of(far, there, other):
        along = (there - 1) * (1 - far % 2) + (tmpls - 1 - there) * (far % 2)
        late = regions + far * (tmpls - 1) + along
        return jnp.where(there == 0, far, late) * subs + other

    mine = rank_of(region, tmpl, sub)
    chans = wave_ref.shape[0] // RES
    pay_rows = chans * SPEC_ROWS + 1
    stride = -(-pay_rows // 8) * 8
    own = group * chans
    total = slots_n * chans
    slots, _, templs = ids_ref.shape
    wide = slots * templs

    def peer(index):
        there, other = index // (blocks * subs), index % subs
        block = index // subs % blocks
        if regions == blocks:
            far = block
            step = lax.rem(region - far + regions, regions)
            block = jnp.where(step == 0, 0, jnp.where(step == regions - 1, 1, 2))
        else:
            step = (0, regions - 1, 1)[block]
            far = lax.rem(region + regions - step, regions)
        back = lax.rem(regions - step, regions)
        back = jnp.where(back == 0, 0, jnp.where(back == regions - 1, 1, 2))
        device = {"region": far, "tmpl": there, "sub": other}
        rank = rank_of(far, there, other)
        twin = jnp.where((there == tmpl) & (other == sub), block, 0)
        return device, rank, block * group + place, back * group + there * subs + other, twin

    def each_peer(action):
        for i in range(slots_n):
            action(*peer(i))

    def slot_rows(slot):
        return recv_ref.at[pl.ds(pl.multiple_of(slot * stride, 8), pay_rows), :]

    def copy_to(slot, device, lane):
        return pltpu.make_async_remote_copy(
            src_ref=slot_rows(place), dst_ref=slot_rows(slot), send_sem=send_sem,
            recv_sem=recv_sem.at[lane], device_id=device, device_id_type=MESH,
        )

    def rows_of(copies):
        return recv_ref.at[pl.ds(0, copies * pay_rows), :]

    barrier = pltpu.get_barrier_semaphore()
    lower = jnp.int32(0)
    for i in range(slots_n):
        device, rank = peer(i)[:2]

        @pl.when(rank > mine)
        def _():
            pl.semaphore_signal(barrier, inc=1, device_id=device, device_id_type=MESH)

        lower += jnp.where(rank < mine, 1, 0)

    start = pl.multiple_of(place * stride, 8)
    lane = lax.broadcasted_iota(jnp.int32, (1, LANES), 1)
    loads[0].wait()
    loads[1].wait()
    high, low = split(wave_ref[...])
    y = dot(gather_ref[...], jnp.concatenate([high, low, high], axis=0))
    half = RES * chans
    loads[2].wait()
    cos, sin = twiddle_ref[:half, :], twiddle_ref[half:, :]
    yr, yi = y[:half], y[half:]
    z = jnp.concatenate([yr * cos + yi * sin, yi * cos - yr * sin], axis=1)
    repeat = lambda x: jnp.concatenate(
        [x[RES * c : RES * (c + 1)] for c in range(chans) for _ in range(COPIES)], axis=0
    )
    high, low = split(z)
    loads[3].wait()
    nt = lambda a, b: lax.dot_general(a, b, ACROSS, preferred_element_type=F32)
    first = nt(steps_ref[...], repeat(high))
    x = first[: 8 * COPIES] + (first[8 * COPIES :] + nt(steps_ref[: 8 * COPIES, :], repeat(low)))
    loads[4].wait()
    loads[5].wait()
    info = start + chans * SPEC_ROWS
    recv_ref[pl.ds(info, 1), :] = jnp.full((1, LANES), -1.0, F32)
    for i, side in enumerate((1, 0)):
        live = lane[:, :bmax] < count_ref[:, side : side + 1]
        listed = jnp.where(live, border_ref[side : side + 1, :], -1).astype(F32)
        recv_ref[pl.ds(info, 1), own + i * bmax : own + (i + 1) * bmax] = listed
    for c in range(chans):
        piece = x[:8, LANES * c : LANES * (c + 1)]
        for k in range(1, COPIES):
            piece = jnp.where(
                lane >= RES * k, x[8 * k : 8 * (k + 1), LANES * c : LANES * (c + 1)], piece
            )
        recv_ref[pl.ds(start + c * SPEC_ROWS, SPEC_ROWS), :] = piece[:SPEC_ROWS]

    @pl.when(lower > 0)
    def _():
        pl.semaphore_wait(barrier, lower)

    def send_down(device, rank, slot, back, twin):
        @pl.when(rank < mine)
        def _():
            copy_to(slot, device, twin).start()

    each_peer(send_down)

    def announce(device, rank, slot, back, twin):
        @pl.when(rank < mine)
        def _():
            pl.semaphore_signal(go_sem.at[slot], inc=1, device_id=device, device_id_type=MESH)

    each_peer(announce)

    loads[6].wait()
    loads[7].wait()
    waves = tmpl_ref[...]
    tspec_ref[...] = dot(waves, short_ref[...])
    waves = waves.astype(F32)
    power = jnp.sum(waves * waves, axis=1, keepdims=True)
    loads[8].wait()
    loads[9].wait()
    square = (templs, templs)
    same = lax.broadcasted_iota(jnp.int32, square, 0) == lax.broadcasted_iota(jnp.int32, square, 1)
    column = lambda x: jnp.sum(jnp.where(same, x, 0), axis=1, keepdims=True, dtype=jnp.int32)
    used = column(active_ref[...])
    id_rows = jnp.concatenate([column(ids_ref[j]) for j in range(slots)], axis=0)
    live = jnp.concatenate([jnp.where(used > j, 1.0, 0.0) for j in range(slots)], axis=0)
    one = lambda mask: jnp.where(mask, 1.0, 0.0).astype(BF16)
    hot_ref[...] = one(id_rows == lane)
    scale = 2.0 / NF * lax.rsqrt(power + EPSILON) * live
    scale_ref[...] = jnp.broadcast_to(scale, (wide, LANES))
    loads[10].wait()
    moves = jnp.concatenate([column(move_ref[j]) for j in range(slots)], axis=0)
    moves_ref[...] = jnp.broadcast_to(moves, (wide, LANES))

    def send_up(device, rank, slot, back, twin):
        @pl.when(rank > mine)
        def _():
            pl.semaphore_wait(go_sem.at[back], 1)
            copy_to(slot, device, twin).start()

    each_peer(send_up)

    left = offsets.index((regions - 1) % regions)
    right = offsets.index(1 % regions)
    far = sorted({b for b in (left, right) if b})
    for b in far:
        copy_to(b * group + place, {"sub": sub}, b).wait_recv()
    listed = lambda b: recv_ref[pl.ds(pl.multiple_of((b * group + place) * stride, 8) + chans * SPEC_ROWS, 1), :].astype(jnp.int32)

    def row_of(b, channel):
        row = lax.rem(channel, chans) * slots_n + b * group + channel // chans
        return jnp.where(channel < 0, -1, row)

    from_left = jnp.where(region > 0, row_of(left, listed(left)), -1)
    from_right = jnp.where(region < regions - 1, row_of(right, listed(right)), -1)
    target = jnp.where(
        lane < own, row_of(0, lane), jnp.where(lane < own + bmax, from_left, from_right)
    )
    row = lax.rem(lax.broadcasted_iota(jnp.int32, (2 * SHIFTS * total, 1), 0), total)
    chosen = lax.dot_general(hot_ref[...], one(row == target), ACROSS, preferred_element_type=F32)
    chosen_ref[...] = chosen[:, : 3 * total].astype(BF16)
    shift = lax.rem(lax.broadcasted_iota(jnp.int32, (1, 2 * SHIFTS * total), 1) // total, SHIFTS)
    weight_ref[...] = jnp.where(shift == moves_ref[:, :1] // LANES, chosen, 0.0).astype(BF16)
    loads[11].wait()
    loads[12].wait()

    others = rows_of(slots_n - 1 - len(far))
    pltpu.make_async_copy(others, others, recv_sem.at[0]).wait()

    table = jnp.concatenate(
        [
            jnp.concatenate(
                [
                    recv_ref[pl.ds(c * SPEC_ROWS + i, slots_n, stride=stride), :]
                    for i in range(SPEC_ROWS)
                ],
                axis=1,
            )
            for c in range(chans)
        ],
        axis=0,
    )
    high = table.astype(BF16)
    rest = table - high.astype(F32)
    middle, low = split(rest)
    parts_ref[...] = jnp.concatenate([high, middle, low], axis=0)
    odd = lax.rem(lax.broadcasted_iota(jnp.int32, (1, 2 * BAND), 1), 2) == 1
    lhs_ref[:total, :] = jnp.where(odd, 0.0, high.astype(F32)).astype(BF16)
    lhs_ref[total : 2 * total, :] = jnp.where(odd, high.astype(F32), 0.0).astype(BF16)
    above = 2 * total
    spec = dot(chosen_ref[...], parts_ref[...])
    xr, xi = spec[:, :BAND], spec[:, BAND:]
    wr, wi = tspec_ref[:, :BAND], tspec_ref[:, BAND:]
    lhs_ref[above:, :BAND] = (wr * xr + wi * xi).astype(BF16)
    lhs_ref[above:, BAND:] = (wr * xi - wi * xr).astype(BF16)
    step = 4 * LANES
    half = slots // 2 * templs
    parts = (slice(0, half), slice(half, wide))
    even, uneven = [], []
    for c in range(0, LN, step):
        corr = dot(lhs_ref[: above + half, :], lag_ref[:, c : c + step])
        even.append(corr[:total])
        uneven.append(corr[total:above])
        corr_ref[parts[0], c : c + step] = corr[above:]
    even, uneven = (jnp.concatenate(x, axis=1) for x in (even, uneven))
    late = even[:, :OUT] - uneven[:, :OUT]
    filtered = 2.0 / NF * jnp.concatenate([even + uneven, late], axis=1)
    power = filtered * filtered
    block = lambda i: power[:, LANES * i : LANES * (i + 1)]
    pieces = jnp.concatenate(
        [
            jnp.concatenate([block(q), block(q + 1) + block(q + 2), block(q + 3), block(q + 4)], axis=1)
            for q in range(BLOCKS)
        ],
        axis=0,
    )

    def correlate(c):
        corr_ref[parts[1], c : c + step] = dot(lhs_ref[above + half :, :], lag_ref[:, c : c + step])

    correlate(0)
    energy = dot(pieces.astype(BF16), window_ref[...])
    for c in range(step, LN, step):
        correlate(c)
    high, middle = split(lax.rsqrt(energy + EPSILON))
    span = SHIFTS * total
    for a in range(OUT // LANES + 1):
        at, rows = slice(LANES * a, LANES * (a + 1)), slice(total * a, total * a + span)
        norms_ref[:span, at] = high[rows]
        norms_ref[span:, at] = middle[rows]

    rows_out = OUT // LANES
    lanes = lax.broadcasted_iota(jnp.int32, (8, LANES), 1)
    scores = [[jnp.zeros((8, LANES), F32)] * rows_out for _ in range(templs // 8)]

    def gather_norms(part):
        near_ref[parts[part], :] = dot(weight_ref[parts[part], :], norms_ref[...])

    def align(j, g):
        rows = slice(j * templs + 8 * g, j * templs + 8 * g + 8)
        move = moves_ref[rows, :]
        odd, far_pair, turn = (move & LANES) != 0, (move & (2 * LANES)) != 0, move & (LANES - 1)
        value = [corr_ref[rows, LANES * i : LANES * (i + 1)] for i in range(BLOCKS)]
        value = [jnp.where(odd, value[i + 1], value[i]) for i in range(BLOCKS - 1)]
        value = [jnp.where(far_pair, value[i + 2], value[i]) for i in range(rows_out + 1)]
        index, near = (lanes + turn) & (LANES - 1), lanes < LANES - turn
        value = [
            jnp.take_along_axis(x * near_ref[rows, LANES * i : LANES * (i + 1)], index, axis=1)
            for i, x in enumerate(value)
        ]
        scale = scale_ref[rows, :]
        for i in range(rows_out):
            scores[g][i] = scores[g][i] + jnp.where(near, value[i], value[i + 1]) * scale

    for part in range(2):
        gather_norms(part)
        for g in range(templs // 8):
            for j in range(slots // 2 * part, slots if part else slots // 2):
                align(j, g)
    for g in range(templs // 8):
        for i in range(rows_out):
            out_ref[8 * g : 8 * g + 8, LANES * i : LANES * (i + 1)] = scores[g][i]

    others = rows_of(slots_n - 1)
    pltpu.make_async_copy(others, others, send_sem).wait()


def on_device(geometry, waveforms, templates, channel_ids, moveouts, active, border, border_count):
    regions, tmpls, subs, offsets = geometry
    slots_n = tmpls * subs * len(offsets)
    chans = waveforms.shape[1]
    bmax = border.shape[2]
    templs, slots = channel_ids.shape[1:]
    wide, total = slots * templs, slots_n * chans
    by_slot = lambda x: jnp.transpose(x, (2, 0, 1))
    short_table, lag_table = wide_tables()
    gather, twiddle, steps, window = small_tables(chans)
    waves = waveforms[0].reshape(chans, RES, LANES).swapaxes(0, 1).reshape(RES * chans, LANES)
    rows = jnp.swapaxes(templates[0], 0, 1).reshape(wide, K)
    inputs = (
        waves, gather, twiddle, steps, border[0], border_count, rows, short_table,
        by_slot(channel_ids), active, by_slot(moveouts), window, lag_table,
    )
    spaces = [pltpu.VMEM] * len(inputs)
    stride = -(-(chans * SPEC_ROWS + 1) // 8) * 8
    vmem = pltpu.VMEM
    scores = pl.pallas_call(
        functools.partial(kernel, geometry, spaces, bmax),
        out_shape=pltpu.VMEM((templs, OUT), F32),
        in_specs=[pl.BlockSpec(memory_space=pltpu.HBM)] * len(inputs),
        out_specs=pl.BlockSpec(memory_space=pltpu.VMEM),
        scratch_shapes=[
            *[space(x.shape, x.dtype) for space, x in zip(spaces, inputs)],
            vmem((slots_n * stride, LANES), F32),
            vmem((wide, 2 * BAND), F32),
            vmem((wide, LANES), BF16),
            vmem((wide, LANES), jnp.int32),
            vmem((wide, 2 * SHIFTS * total), BF16),
            vmem((wide, 3 * total), BF16),
            vmem((3 * total, 2 * BAND), BF16),
            vmem((2 * SHIFTS * total, OUT + LANES), BF16),
            vmem((2 * total + wide, 2 * BAND), BF16),
            vmem((wide, LN), F32),
            vmem((wide, OUT + LANES), F32),
            vmem((wide, LANES), F32),
            pltpu.SemaphoreType.DMA((len(inputs),)),
            pltpu.SemaphoreType.DMA,
            pltpu.SemaphoreType.DMA((len(offsets),)),
            pltpu.SemaphoreType.REGULAR((slots_n,)),
        ],
        compiler_params=pltpu.CompilerParams(
            collective_id=0, has_side_effects=True
        ),
        name="detect",
    )(*inputs)
    return scores[None]


def solution(mesh):
    regions, tmpls, subs = (mesh.shape[a] for a in ("region", "tmpl", "sub"))
    offsets = tuple(dict.fromkeys((0, (regions - 1) % regions, 1 % regions)))
    geometry = (regions, tmpls, subs, offsets)
    in_specs = (
        P("region", ("tmpl", "sub"), "groups"),
        P("region", ("tmpl", "sub"), None, None),
        P("region", ("tmpl", "sub"), None),
        P("region", ("tmpl", "sub"), None),
        P("region", ("tmpl", "sub")),
        P("region", None, None),
        P("region", None),
    )
    return jax.shard_map(
        functools.partial(on_device, geometry),
        mesh=mesh,
        in_specs=in_specs,
        out_specs=P("region", ("tmpl", "sub"), "groups"),
        check_vma=False,
    )
```

```python
import functools

import jax
import jax.numpy as jnp
import ml_dtypes
import numpy as np
from jax import lax
from jax.experimental import pallas as pl
from jax.experimental.pallas import tpu as pltpu
from jax.sharding import PartitionSpec as P

NF = 2048
F0 = 40
BAND = 384
K = 400
OUT = 512
LN = 1024
EPSILON = 1e-06

LANES = 128
RES = NF // LANES
STEPS = BAND // RES
COPIES = LANES // RES
PART = STEPS // COPIES
SPEC_ROWS = 2 * PART
BLOCKS = LN // LANES
SHIFTS = BLOCKS - OUT // LANES
MESH = pl.DeviceIdType.MESH
TURN = 2.0 * np.pi / NF
BF16, F32 = jnp.bfloat16, jnp.float32
ACROSS = (((1,), (1,)), ((), ()))


def as_bf16(x):
    return x.astype(np.float32).astype(ml_dtypes.bfloat16)


def halves(x):
    x = x.astype(np.float32)
    high = x.astype(ml_dtypes.bfloat16)
    return high, (x - high.astype(np.float32)).astype(ml_dtypes.bfloat16)


def bin_order():
    i, k, r = np.meshgrid(np.arange(PART), np.arange(COPIES), np.arange(RES), indexing="ij")
    return (F0 + RES * (PART * k + i) + r).reshape(-1)


def wide_tables():
    bins = bin_order()
    short = (np.arange(K)[:, None] * bins[None, :] % NF) * TURN
    short = np.concatenate([np.cos(short), -np.sin(short)], axis=1)
    lag = (bins[:, None] * np.arange(LN)[None, :] % NF) * TURN
    lag = np.concatenate([np.cos(lag), -np.sin(lag)], axis=0)
    return as_bf16(short), as_bf16(lag)


def small_tables(chans):
    r, a, b = np.arange(RES), np.arange(RES), np.arange(LANES)
    alpha = (F0 + r)[:, None] * a[None, :] * LANES % NF * TURN
    spread = lambda x: np.einsum("ra,cd->crad", x, np.eye(chans)).reshape(chans * RES, RES * chans)
    high, low = halves(np.concatenate([spread(np.cos(alpha)), spread(-np.sin(alpha))], axis=0))
    gather = np.concatenate([high, high, low], axis=1)
    theta = np.tile((F0 + r)[:, None] * b[None, :] % NF * TURN, (chans, 1))
    twiddle = np.concatenate([np.cos(theta), np.sin(theta)], axis=0).astype(np.float32)
    rows = np.zeros((COPIES, 8, 2 * LANES))
    for k in range(COPIES):
        beta = (PART * k + np.arange(PART))[:, None] * b[None, :] * RES % NF * TURN
        rows[k, :PART] = np.concatenate([np.cos(beta), np.sin(beta)], axis=1)
        rows[k, PART : 2 * PART] = np.concatenate([-np.sin(beta), np.cos(beta)], axis=1)
    steps = np.concatenate(halves(rows.reshape(8 * COPIES, 2 * LANES)), axis=0)
    window = []
    for i in (0, 1, 3, 4):
        place = LANES * i + b[:, None] - b[None, :]
        window.append((place >= 0) & (place < K))
    return gather, twiddle, steps, as_bf16(np.concatenate(window, axis=0))


def split(x):
    high = x.astype(BF16)
    return high, (x - high.astype(F32)).astype(BF16)


def dot(a, b):
    return jnp.dot(a, b, preferred_element_type=F32)


def kernel(geometry, spaces, bmax, *refs):
    count = len(spaces)
    hbm, out_ref, local = refs[:count], refs[count], refs[count + 1 : 2 * count + 1]
    (
        recv_ref, tspec_ref, hot_ref, moves_ref, weight_ref, chosen_ref, parts_ref, norms_ref,
        lhs_ref, corr_ref, near_ref, scale_ref, load_sem, send_sem, recv_sem, go_sem,
    ) = refs[2 * count + 1 :]
    loads = [pltpu.make_async_copy(h, v, load_sem.at[i]) for i, (h, v) in enumerate(zip(hbm, local))]
    for load in loads:
        load.start()
    (
        wave_ref, gather_ref, twiddle_ref, steps_ref, border_ref, count_ref, tmpl_ref, short_ref,
        ids_ref, active_ref, move_ref, window_ref, lag_ref,
    ) = local
    regions, tmpls, subs, offsets = geometry
    group, blocks = tmpls * subs, len(offsets)
    slots_n = group * blocks
    region, tmpl, sub = (lax.axis_index(a) for a in ("region", "tmpl", "sub"))
    place = tmpl * subs + sub

    def rank_of(far, there, other):
        along = (there - 1) * (1 - far % 2) + (tmpls - 1 - there) * (far % 2)
        late = regions + far * (tmpls - 1) + along
        return jnp.where(there == 0, far, late) * subs + other

    mine = rank_of(region, tmpl, sub)
    chans = wave_ref.shape[0] // RES
    pay_rows = chans * SPEC_ROWS + 1
    stride = -(-pay_rows // 8) * 8
    own = group * chans
    total = slots_n * chans
    slots, _, templs = ids_ref.shape
    wide = slots * templs

    def peer(index):
        there, other = index // (blocks * subs), index % subs
        block = index // subs % blocks
        if regions == blocks:
            far = block
            step = lax.rem(region - far + regions, regions)
            block = jnp.where(step == 0, 0, jnp.where(step == regions - 1, 1, 2))
        else:
            step = (0, regions - 1, 1)[block]
            far = lax.rem(region + regions - step, regions)
        back = lax.rem(regions - step, regions)
        back = jnp.where(back == 0, 0, jnp.where(back == regions - 1, 1, 2))
        device = {"region": far, "tmpl": there, "sub": other}
        rank = rank_of(far, there, other)
        twin = block + jnp.where((there == tmpl) & (other == sub) & (block > 0), blocks - 1, 0)
        return device, rank, block * group + place, back * group + there * subs + other, twin

    def each_peer(action):
        for i in range(slots_n):
            action(*peer(i))

    def slot_rows(slot):
        return recv_ref.at[pl.ds(pl.multiple_of(slot * stride, 8), pay_rows), :]

    def copy_to(slot, device, lane):
        return pltpu.make_async_remote_copy(
            src_ref=slot_rows(place), dst_ref=slot_rows(slot), send_sem=send_sem,
            recv_sem=recv_sem.at[lane], device_id=device, device_id_type=MESH,
        )

    def rows_of(copies):
        return recv_ref.at[pl.ds(0, copies * pay_rows), :]

    barrier = pltpu.get_barrier_semaphore()
    lower = jnp.int32(0)
    for i in range(slots_n):
        device, rank = peer(i)[:2]

        @pl.when(rank > mine)
        def _():
            pl.semaphore_signal(barrier, inc=1, device_id=device, device_id_type=MESH)

        lower += jnp.where(rank < mine, 1, 0)

    start = pl.multiple_of(place * stride, 8)
    lane = lax.broadcasted_iota(jnp.int32, (1, LANES), 1)
    loads[0].wait()
    loads[1].wait()
    high, low = split(wave_ref[...])
    y = dot(gather_ref[...], jnp.concatenate([high, low, high], axis=0))
    half = RES * chans
    loads[2].wait()
    cos, sin = twiddle_ref[:half, :], twiddle_ref[half:, :]
    yr, yi = y[:half], y[half:]
    z = jnp.concatenate([yr * cos + yi * sin, yi * cos - yr * sin], axis=1)
    repeat = lambda x: jnp.concatenate(
        [x[RES * c : RES * (c + 1)] for c in range(chans) for _ in range(COPIES)], axis=0
    )
    high, low = split(z)
    loads[3].wait()
    nt = lambda a, b: lax.dot_general(a, b, ACROSS, preferred_element_type=F32)
    first = nt(steps_ref[...], repeat(high))
    x = first[: 8 * COPIES] + (first[8 * COPIES :] + nt(steps_ref[: 8 * COPIES, :], repeat(low)))
    loads[4].wait()
    loads[5].wait()
    info = start + chans * SPEC_ROWS
    recv_ref[pl.ds(info, 1), :] = jnp.full((1, LANES), -1.0, F32)
    for i, side in enumerate((1, 0)):
        live = lane[:, :bmax] < count_ref[:, side : side + 1]
        listed = jnp.where(live, border_ref[side : side + 1, :], -1).astype(F32)
        recv_ref[pl.ds(info, 1), own + i * bmax : own + (i + 1) * bmax] = listed
    for c in range(chans):
        piece = x[:8, LANES * c : LANES * (c + 1)]
        for k in range(1, COPIES):
            piece = jnp.where(
                lane >= RES * k, x[8 * k : 8 * (k + 1), LANES * c : LANES * (c + 1)], piece
            )
        recv_ref[pl.ds(start + c * SPEC_ROWS, SPEC_ROWS), :] = piece[:SPEC_ROWS]

    @pl.when(lower > 0)
    def _():
        pl.semaphore_wait(barrier, lower)

    def send_down(device, rank, slot, back, twin):
        @pl.when(rank < mine)
        def _():
            copy_to(slot, device, twin).start()

    each_peer(send_down)

    def announce(device, rank, slot, back, twin):
        @pl.when(rank < mine)
        def _():
            pl.semaphore_signal(go_sem.at[slot], inc=1, device_id=device, device_id_type=MESH)

    each_peer(announce)

    loads[6].wait()
    loads[7].wait()
    waves = tmpl_ref[...]
    tspec_ref[...] = dot(waves, short_ref[...])
    waves = waves.astype(F32)
    power = jnp.sum(waves * waves, axis=1, keepdims=True)
    loads[8].wait()
    loads[9].wait()
    square = (templs, templs)
    same = lax.broadcasted_iota(jnp.int32, square, 0) == lax.broadcasted_iota(jnp.int32, square, 1)
    column = lambda x: jnp.sum(jnp.where(same, x, 0), axis=1, keepdims=True, dtype=jnp.int32)
    used = column(active_ref[...])
    id_rows = jnp.concatenate([column(ids_ref[j]) for j in range(slots)], axis=0)
    live = jnp.concatenate([jnp.where(used > j, 1.0, 0.0) for j in range(slots)], axis=0)
    one = lambda mask: jnp.where(mask, 1.0, 0.0).astype(BF16)
    hot_ref[...] = one(id_rows == lane)
    scale = 2.0 / NF * lax.rsqrt(power + EPSILON) * live
    scale_ref[...] = jnp.broadcast_to(scale, (wide, LANES))
    loads[10].wait()
    moves = jnp.concatenate([column(move_ref[j]) for j in range(slots)], axis=0)
    moves_ref[...] = jnp.broadcast_to(moves, (wide, LANES))

    def send_up(device, rank, slot, back, twin):
        @pl.when(rank > mine)
        def _():
            pl.semaphore_wait(go_sem.at[back], 1)
            copy_to(slot, device, twin).start()

    each_peer(send_up)

    left = offsets.index((regions - 1) % regions)
    right = offsets.index(1 % regions)
    far = sorted({b for b in (left, right) if b})
    for b in far:
        copy_to(b * group + place, {"sub": sub}, blocks - 1 + b).wait_recv()
    listed = lambda b: recv_ref[pl.ds(pl.multiple_of((b * group + place) * stride, 8) + chans * SPEC_ROWS, 1), :].astype(jnp.int32)

    def row_of(b, channel):
        row = b * own + lax.rem(channel, chans) * group + channel // chans
        return jnp.where(channel < 0, -1, row)

    from_left = jnp.where(region > 0, row_of(left, listed(left)), -1)
    from_right = jnp.where(region < regions - 1, row_of(right, listed(right)), -1)
    target = jnp.where(
        lane < own, row_of(0, lane), jnp.where(lane < own + bmax, from_left, from_right)
    )
    row = lax.rem(lax.broadcasted_iota(jnp.int32, (2 * SHIFTS * total, 1), 0), total)
    chosen = lax.dot_general(hot_ref[...], one(row == target), ACROSS, preferred_element_type=F32)
    chosen_ref[...] = chosen[:, : 3 * total].astype(BF16)
    shift = lax.rem(lax.broadcasted_iota(jnp.int32, (1, 2 * SHIFTS * total), 1) // total, SHIFTS)
    weight_ref[...] = jnp.where(shift == moves_ref[:, :1] // LANES, chosen, 0.0).astype(BF16)
    loads[11].wait()
    loads[12].wait()

    odd = lax.rem(lax.broadcasted_iota(jnp.int32, (1, 2 * BAND), 1), 2) == 1
    for b in range(blocks):
        others = rows_of(group - 1)
        pltpu.make_async_copy(others, others, recv_sem.at[b]).wait()
        first = b * group * stride
        table = jnp.concatenate(
            [
                jnp.concatenate(
                    [
                        recv_ref[pl.ds(first + c * SPEC_ROWS + i, group, stride=stride), :]
                        for i in range(SPEC_ROWS)
                    ],
                    axis=1,
                )
                for c in range(chans)
            ],
            axis=0,
        )
        high = table.astype(BF16)
        rest = table - high.astype(F32)
        at = b * own
        for value in (high, *split(rest)):
            parts_ref[at : at + own, :] = value
            at += total
        at, high = slice(b * own, (b + 1) * own), high.astype(F32)
        lhs_ref[at, :] = jnp.where(odd, 0.0, high).astype(BF16)
        lhs_ref[total + b * own : total + (b + 1) * own, :] = jnp.where(odd, high, 0.0).astype(BF16)
    above = 2 * total
    spec = dot(chosen_ref[...], parts_ref[...])
    xr, xi = spec[:, :BAND], spec[:, BAND:]
    wr, wi = tspec_ref[:, :BAND], tspec_ref[:, BAND:]
    lhs_ref[above:, :BAND] = (wr * xr + wi * xi).astype(BF16)
    lhs_ref[above:, BAND:] = (wr * xi - wi * xr).astype(BF16)
    step = 4 * LANES
    half = slots // 2 * templs
    parts = (slice(0, half), slice(half, wide))
    even, uneven = [], []
    for c in range(0, LN, step):
        corr = dot(lhs_ref[: above + half, :], lag_ref[:, c : c + step])
        even.append(corr[:total])
        uneven.append(corr[total:above])
        corr_ref[parts[0], c : c + step] = corr[above:]
    even, uneven = (jnp.concatenate(x, axis=1) for x in (even, uneven))
    late = even[:, :OUT] - uneven[:, :OUT]
    filtered = 2.0 / NF * jnp.concatenate([even + uneven, late], axis=1)
    power = filtered * filtered
    block = lambda i: power[:, LANES * i : LANES * (i + 1)]
    pieces = jnp.concatenate(
        [
            jnp.concatenate([block(q), block(q + 1) + block(q + 2), block(q + 3), block(q + 4)], axis=1)
            for q in range(BLOCKS)
        ],
        axis=0,
    )

    def correlate(c):
        corr_ref[parts[1], c : c + step] = dot(lhs_ref[above + half :, :], lag_ref[:, c : c + step])

    correlate(0)
    energy = dot(pieces.astype(BF16), window_ref[...])
    for c in range(step, LN, step):
        correlate(c)
    high, middle = split(lax.rsqrt(energy + EPSILON))
    span = SHIFTS * total
    for a in range(OUT // LANES + 1):
        at, rows = slice(LANES * a, LANES * (a + 1)), slice(total * a, total * a + span)
        norms_ref[:span, at] = high[rows]
        norms_ref[span:, at] = middle[rows]

    rows_out = OUT // LANES
    lanes = lax.broadcasted_iota(jnp.int32, (8, LANES), 1)
    scores = [[jnp.zeros((8, LANES), F32)] * rows_out for _ in range(templs // 8)]

    def gather_norms(part):
        near_ref[parts[part], :] = dot(weight_ref[parts[part], :], norms_ref[...])

    def align(j, g):
        rows = slice(j * templs + 8 * g, j * templs + 8 * g + 8)
        move = moves_ref[rows, :]
        odd, far_pair, turn = (move & LANES) != 0, (move & (2 * LANES)) != 0, move & (LANES - 1)
        value = [corr_ref[rows, LANES * i : LANES * (i + 1)] for i in range(BLOCKS)]
        value = [jnp.where(odd, value[i + 1], value[i]) for i in range(BLOCKS - 1)]
        value = [jnp.where(far_pair, value[i + 2], value[i]) for i in range(rows_out + 1)]
        index, near = (lanes + turn) & (LANES - 1), lanes < LANES - turn
        value = [
            jnp.take_along_axis(x * near_ref[rows, LANES * i : LANES * (i + 1)], index, axis=1)
            for i, x in enumerate(value)
        ]
        scale = scale_ref[rows, :]
        for i in range(rows_out):
            scores[g][i] = scores[g][i] + jnp.where(near, value[i], value[i + 1]) * scale

    for part in range(2):
        gather_norms(part)
        for g in range(templs // 8):
            for j in range(slots // 2 * part, slots if part else slots // 2):
                align(j, g)
    for g in range(templs // 8):
        for i in range(rows_out):
            out_ref[8 * g : 8 * g + 8, LANES * i : LANES * (i + 1)] = scores[g][i]

    others = rows_of(slots_n - 1)
    pltpu.make_async_copy(others, others, send_sem).wait()


def on_device(geometry, waveforms, templates, channel_ids, moveouts, active, border, border_count):
    regions, tmpls, subs, offsets = geometry
    slots_n = tmpls * subs * len(offsets)
    chans = waveforms.shape[1]
    bmax = border.shape[2]
    templs, slots = channel_ids.shape[1:]
    wide, total = slots * templs, slots_n * chans
    by_slot = lambda x: jnp.transpose(x, (2, 0, 1))
    short_table, lag_table = wide_tables()
    gather, twiddle, steps, window = small_tables(chans)
    waves = waveforms[0].reshape(chans, RES, LANES).swapaxes(0, 1).reshape(RES * chans, LANES)
    rows = jnp.swapaxes(templates[0], 0, 1).reshape(wide, K)
    inputs = (
        waves, gather, twiddle, steps, border[0], border_count, rows, short_table,
        by_slot(channel_ids), active, by_slot(moveouts), window, lag_table,
    )
    spaces = [pltpu.VMEM] * len(inputs)
    stride = -(-(chans * SPEC_ROWS + 1) // 8) * 8
    vmem = pltpu.VMEM
    scores = pl.pallas_call(
        functools.partial(kernel, geometry, spaces, bmax),
        out_shape=pltpu.VMEM((templs, OUT), F32),
        in_specs=[pl.BlockSpec(memory_space=pltpu.HBM)] * len(inputs),
        out_specs=pl.BlockSpec(memory_space=pltpu.VMEM),
        scratch_shapes=[
            *[space(x.shape, x.dtype) for space, x in zip(spaces, inputs)],
            vmem((slots_n * stride, LANES), F32),
            vmem((wide, 2 * BAND), F32),
            vmem((wide, LANES), BF16),
            vmem((wide, LANES), jnp.int32),
            vmem((wide, 2 * SHIFTS * total), BF16),
            vmem((wide, 3 * total), BF16),
            vmem((3 * total, 2 * BAND), BF16),
            vmem((2 * SHIFTS * total, OUT + LANES), BF16),
            vmem((2 * total + wide, 2 * BAND), BF16),
            vmem((wide, LN), F32),
            vmem((wide, OUT + LANES), F32),
            vmem((wide, LANES), F32),
            pltpu.SemaphoreType.DMA((len(inputs),)),
            pltpu.SemaphoreType.DMA,
            pltpu.SemaphoreType.DMA((2 * len(offsets) - 1,)),
            pltpu.SemaphoreType.REGULAR((slots_n,)),
        ],
        compiler_params=pltpu.CompilerParams(
            collective_id=0, has_side_effects=True
        ),
        name="detect",
    )(*inputs)
    return scores[None]


def solution(mesh):
    regions, tmpls, subs = (mesh.shape[a] for a in ("region", "tmpl", "sub"))
    offsets = tuple(dict.fromkeys((0, (regions - 1) % regions, 1 % regions)))
    geometry = (regions, tmpls, subs, offsets)
    in_specs = (
        P("region", ("tmpl", "sub"), "groups"),
        P("region", ("tmpl", "sub"), None, None),
        P("region", ("tmpl", "sub"), None),
        P("region", ("tmpl", "sub"), None),
        P("region", ("tmpl", "sub")),
        P("region", None, None),
        P("region", None),
    )
    return jax.shard_map(
        functools.partial(on_device, geometry),
        mesh=mesh,
        in_specs=in_specs,
        out_specs=P("region", ("tmpl", "sub"), "groups"),
        check_vma=False,
    )
```

```python
import functools

import jax
import jax.numpy as jnp
import ml_dtypes
import numpy as np
from jax import lax
from jax.experimental import pallas as pl
from jax.experimental.pallas import tpu as pltpu
from jax.sharding import PartitionSpec as P

NF = 2048
F0 = 40
BAND = 384
K = 400
OUT = 512
LN = 1024
EPSILON = 1e-06

LANES = 128
RES = NF // LANES
STEPS = BAND // RES
COPIES = LANES // RES
PART = STEPS // COPIES
SPEC_ROWS = 2 * PART
BLOCKS = LN // LANES
SPAN = LN + OUT
MESH = pl.DeviceIdType.MESH
TURN = 2.0 * np.pi / NF
BF16, F32 = jnp.bfloat16, jnp.float32
ACROSS = (((1,), (1,)), ((), ()))


def as_bf16(x):
    return x.astype(np.float32).astype(ml_dtypes.bfloat16)


def halves(x):
    x = x.astype(np.float32)
    high = x.astype(ml_dtypes.bfloat16)
    return high, (x - high.astype(np.float32)).astype(ml_dtypes.bfloat16)


def bin_order():
    i, k, r = np.meshgrid(np.arange(PART), np.arange(COPIES), np.arange(RES), indexing="ij")
    return (F0 + RES * (PART * k + i) + r).reshape(-1)


def wide_tables():
    bins = bin_order()
    short = (np.arange(K)[:, None] * bins[None, :] % NF) * TURN
    short = np.concatenate([np.cos(short), -np.sin(short)], axis=1)
    lag = (bins[:, None] * np.arange(SPAN)[None, :] % NF) * TURN
    lag = np.concatenate([np.cos(lag), -np.sin(lag)], axis=0)
    return as_bf16(short), as_bf16(lag)


def small_tables(chans):
    r, a, b = np.arange(RES), np.arange(RES), np.arange(LANES)
    alpha = (F0 + r)[:, None] * a[None, :] * LANES % NF * TURN
    spread = lambda x: np.einsum("ra,cd->crad", x, np.eye(chans)).reshape(chans * RES, RES * chans)
    high, low = halves(np.concatenate([spread(np.cos(alpha)), spread(-np.sin(alpha))], axis=0))
    gather = np.concatenate([high, high, low], axis=1)
    theta = np.tile((F0 + r)[:, None] * b[None, :] % NF * TURN, (chans, 1))
    twiddle = np.concatenate([np.cos(theta), np.sin(theta)], axis=0).astype(np.float32)
    rows = np.zeros((COPIES, 8, 2 * LANES))
    for k in range(COPIES):
        beta = (PART * k + np.arange(PART))[:, None] * b[None, :] * RES % NF * TURN
        rows[k, :PART] = np.concatenate([np.cos(beta), np.sin(beta)], axis=1)
        rows[k, PART : 2 * PART] = np.concatenate([-np.sin(beta), np.cos(beta)], axis=1)
    steps = np.concatenate(halves(rows.reshape(8 * COPIES, 2 * LANES)), axis=0)
    window = []
    for i in (0, 1, 3, 4):
        place = LANES * i + b[:, None] - b[None, :]
        window.append((place >= 0) & (place < K))
    return gather, twiddle, steps, as_bf16(np.concatenate(window, axis=0))


def split(x):
    high = x.astype(BF16)
    return high, (x - high.astype(F32)).astype(BF16)


def dot(a, b):
    return jnp.dot(a, b, preferred_element_type=F32)


def kernel(geometry, spaces, bmax, *refs):
    count = len(spaces)
    hbm, out_ref, local = refs[:count], refs[count], refs[count + 1 : 2 * count + 1]
    (
        recv_ref, tspec_ref, hot_ref, moves_ref, weight_ref, chosen_ref, parts_ref, norms_ref,
        lhs_ref, corr_ref, load_sem, send_sem, recv_sem, go_sem,
    ) = refs[2 * count + 1 :]
    loads = [pltpu.make_async_copy(h, v, load_sem.at[i]) for i, (h, v) in enumerate(zip(hbm, local))]
    for load in loads:
        load.start()
    (
        wave_ref, gather_ref, twiddle_ref, steps_ref, border_ref, count_ref, tmpl_ref, short_ref,
        ids_ref, active_ref, move_ref, window_ref, lag_ref,
    ) = local
    regions, tmpls, subs, offsets = geometry
    group, blocks = tmpls * subs, len(offsets)
    slots_n = group * blocks
    region, tmpl, sub = (lax.axis_index(a) for a in ("region", "tmpl", "sub"))
    place = tmpl * subs + sub

    def rank_of(far, there, other):
        along = (there - 1) * (1 - far % 2) + (tmpls - 1 - there) * (far % 2)
        late = regions + far * (tmpls - 1) + along
        return jnp.where(there == 0, far, late) * subs + other

    mine = rank_of(region, tmpl, sub)
    chans = wave_ref.shape[0] // RES
    pay_rows = chans * SPEC_ROWS + 1
    stride = -(-pay_rows // 8) * 8
    own = group * chans
    total = slots_n * chans
    slots, _, templs = ids_ref.shape
    wide = slots * templs

    def peer(index):
        there, other = index // (blocks * subs), index % subs
        block = index // subs % blocks
        if regions == blocks:
            far = block
            step = lax.rem(region - far + regions, regions)
            block = jnp.where(step == 0, 0, jnp.where(step == regions - 1, 1, 2))
        else:
            step = (0, regions - 1, 1)[block]
            far = lax.rem(region + regions - step, regions)
        back = lax.rem(regions - step, regions)
        back = jnp.where(back == 0, 0, jnp.where(back == regions - 1, 1, 2))
        device = {"region": far, "tmpl": there, "sub": other}
        rank = rank_of(far, there, other)
        twin = jnp.where((there == tmpl) & (other == sub), block, 0)
        return device, rank, block * group + place, back * group + there * subs + other, twin

    def each_peer(action):
        for i in range(slots_n):
            action(*peer(i))

    def slot_rows(slot):
        return recv_ref.at[pl.ds(pl.multiple_of(slot * stride, 8), pay_rows), :]

    def copy_to(slot, device, lane):
        return pltpu.make_async_remote_copy(
            src_ref=slot_rows(place), dst_ref=slot_rows(slot), send_sem=send_sem,
            recv_sem=recv_sem.at[lane], device_id=device, device_id_type=MESH,
        )

    def rows_of(copies):
        return recv_ref.at[pl.ds(0, copies * pay_rows), :]

    barrier = pltpu.get_barrier_semaphore()
    lower = jnp.int32(0)
    for i in range(slots_n):
        device, rank = peer(i)[:2]

        @pl.when(rank > mine)
        def _():
            pl.semaphore_signal(barrier, inc=1, device_id=device, device_id_type=MESH)

        lower += jnp.where(rank < mine, 1, 0)

    start = pl.multiple_of(place * stride, 8)
    loads[4].wait()
    loads[5].wait()
    lane = lax.broadcasted_iota(jnp.int32, (1, LANES), 1)
    info = start + chans * SPEC_ROWS
    recv_ref[pl.ds(info, 1), :] = jnp.full((1, LANES), -1.0, F32)
    for i, side in enumerate((1, 0)):
        live = lane[:, :bmax] < count_ref[:, side : side + 1]
        listed = jnp.where(live, border_ref[side : side + 1, :], -1).astype(F32)
        recv_ref[pl.ds(info, 1), own + i * bmax : own + (i + 1) * bmax] = listed

    loads[0].wait()
    loads[1].wait()
    high, low = split(wave_ref[...])
    y = dot(gather_ref[...], jnp.concatenate([high, low, high], axis=0))
    half = RES * chans
    loads[2].wait()
    cos, sin = twiddle_ref[:half, :], twiddle_ref[half:, :]
    yr, yi = y[:half], y[half:]
    z = jnp.concatenate([yr * cos + yi * sin, yi * cos - yr * sin], axis=1)
    repeat = lambda x: jnp.concatenate(
        [x[RES * c : RES * (c + 1)] for c in range(chans) for _ in range(COPIES)], axis=0
    )
    high, low = split(z)
    loads[3].wait()
    nt = lambda a, b: lax.dot_general(a, b, ACROSS, preferred_element_type=F32)
    first = nt(steps_ref[...], repeat(high))
    x = first[: 8 * COPIES] + (first[8 * COPIES :] + nt(steps_ref[: 8 * COPIES, :], repeat(low)))
    for c in range(chans):
        piece = x[:8, LANES * c : LANES * (c + 1)]
        for k in range(1, COPIES):
            piece = jnp.where(
                lane >= RES * k, x[8 * k : 8 * (k + 1), LANES * c : LANES * (c + 1)], piece
            )
        recv_ref[pl.ds(start + c * SPEC_ROWS, SPEC_ROWS), :] = piece[:SPEC_ROWS]

    @pl.when(lower > 0)
    def _():
        pl.semaphore_wait(barrier, lower)

    def send_down(device, rank, slot, back, twin):
        @pl.when(rank < mine)
        def _():
            copy_to(slot, device, twin).start()

    each_peer(send_down)

    def announce(device, rank, slot, back, twin):
        @pl.when(rank < mine)
        def _():
            pl.semaphore_signal(go_sem.at[slot], inc=1, device_id=device, device_id_type=MESH)

    each_peer(announce)

    loads[6].wait()
    loads[7].wait()
    waves = tmpl_ref[...]
    tspec_ref[...] = dot(waves, short_ref[...])
    waves = waves.astype(F32)
    power = jnp.sum(waves * waves, axis=1, keepdims=True)
    loads[8].wait()
    loads[9].wait()
    square = (templs, templs)
    same = lax.broadcasted_iota(jnp.int32, square, 0) == lax.broadcasted_iota(jnp.int32, square, 1)
    column = lambda x: jnp.sum(jnp.where(same, x, 0), axis=1, keepdims=True, dtype=jnp.int32)
    used = column(active_ref[...])
    id_rows = jnp.concatenate([column(ids_ref[j]) for j in range(slots)], axis=0)
    live = jnp.concatenate([jnp.where(used > j, 1.0, 0.0) for j in range(slots)], axis=0)
    one = lambda mask: jnp.where(mask, 1.0, 0.0).astype(BF16)
    hot_ref[...] = one(id_rows == lane)
    scale = 2.0 / NF * lax.rsqrt(power + EPSILON) * live
    scale_high = scale.astype(BF16).astype(F32)
    part = lax.broadcasted_iota(jnp.int32, (1, 3 * total), 1)
    weight_ref[...] = jnp.where(part < 2 * total, scale_high, scale - scale_high).astype(BF16)
    loads[10].wait()
    moves = jnp.concatenate([column(move_ref[j]) for j in range(slots)], axis=0)
    moves_ref[...] = jnp.broadcast_to(moves, (wide, LANES))

    def send_up(device, rank, slot, back, twin):
        @pl.when(rank > mine)
        def _():
            pl.semaphore_wait(go_sem.at[back], 1)
            copy_to(slot, device, twin).start()

    each_peer(send_up)

    left = offsets.index((regions - 1) % regions)
    right = offsets.index(1 % regions)
    far = sorted({b for b in (left, right) if b})
    for b in far:
        copy_to(b * group + place, {"sub": sub}, b).wait_recv()
    listed = lambda b: recv_ref[pl.ds(pl.multiple_of((b * group + place) * stride, 8) + chans * SPEC_ROWS, 1), :].astype(jnp.int32)

    def row_of(b, channel):
        row = lax.rem(channel, chans) * slots_n + b * group + channel // chans
        return jnp.where(channel < 0, -1, row)

    from_left = jnp.where(region > 0, row_of(left, listed(left)), -1)
    from_right = jnp.where(region < regions - 1, row_of(right, listed(right)), -1)
    target = jnp.where(
        lane < own, row_of(0, lane), jnp.where(lane < own + bmax, from_left, from_right)
    )
    row = lax.rem(lax.broadcasted_iota(jnp.int32, (3 * total, 1), 0), total)
    chosen = lax.dot_general(hot_ref[...], one(row == target), ACROSS, preferred_element_type=F32)
    chosen_ref[...] = chosen.astype(BF16)
    weight_ref[...] = (chosen * weight_ref[...].astype(F32)).astype(BF16)
    loads[11].wait()
    loads[12].wait()

    others = rows_of(slots_n - 1 - len(far))
    pltpu.make_async_copy(others, others, recv_sem.at[0]).wait()

    table = jnp.concatenate(
        [
            jnp.concatenate(
                [
                    recv_ref[pl.ds(c * SPEC_ROWS + i, slots_n, stride=stride), :]
                    for i in range(SPEC_ROWS)
                ],
                axis=1,
            )
            for c in range(chans)
        ],
        axis=0,
    )
    high = table.astype(BF16)
    rest = table - high.astype(F32)
    middle, low = split(rest)
    parts_ref[...] = jnp.concatenate([high, middle, low], axis=0)
    lhs_ref[:total, :] = high
    spec = dot(chosen_ref[...], parts_ref[...])
    late = dot(high, lag_ref[:, LN:])
    xr, xi = spec[:, :BAND], spec[:, BAND:]
    wr, wi = tspec_ref[:, :BAND], tspec_ref[:, BAND:]
    lhs_ref[total:, :BAND] = (wr * xr + wi * xi).astype(BF16)
    lhs_ref[total:, BAND:] = (wr * xi - wi * xr).astype(BF16)
    step = 8 * LANES
    half = slots // 2 * templs
    parts = (slice(0, half), slice(half, wide))
    filtered = []
    for c in range(0, LN, step):
        corr = dot(lhs_ref[: total + half, :], lag_ref[:, c : c + step])
        filtered.append(corr[:total])
        corr_ref[parts[0], c : c + step] = corr[total:]
    filtered = 2.0 / NF * jnp.concatenate([*filtered, late], axis=1)
    power = filtered * filtered
    block = lambda i: power[:, LANES * i : LANES * (i + 1)]
    pieces = jnp.concatenate(
        [
            jnp.concatenate([block(q), block(q + 1) + block(q + 2), block(q + 3), block(q + 4)], axis=1)
            for q in range(BLOCKS)
        ],
        axis=0,
    )

    def correlate(c):
        corr_ref[parts[1], c : c + step] = dot(lhs_ref[total + half :, :], lag_ref[:, c : c + step])

    energy = dot(pieces.astype(BF16), window_ref[...])
    correlate(0)
    high, middle = split(lax.rsqrt(energy + EPSILON))
    for q in range(BLOCKS):
        at, rows = slice(LANES * q, LANES * (q + 1)), slice(total * q, total * (q + 1))
        norms_ref[:total, at] = high[rows]
        norms_ref[total : 2 * total, at] = middle[rows]
        norms_ref[2 * total :, at] = high[rows]

    rows_out = OUT // LANES
    lanes = lax.broadcasted_iota(jnp.int32, (8, LANES), 1)
    scores = [[jnp.zeros((8, LANES), F32)] * rows_out for _ in range(templs // 8)]

    def normalise(part, c):
        at = slice(c, c + step)
        corr_ref[parts[part], at] *= dot(weight_ref[parts[part], :], norms_ref[:, at])

    def align(j, g):
        rows = slice(j * templs + 8 * g, j * templs + 8 * g + 8)
        move = moves_ref[rows, :]
        odd, far_pair, turn = (move & LANES) != 0, (move & (2 * LANES)) != 0, move & (LANES - 1)
        value = [corr_ref[rows, LANES * i : LANES * (i + 1)] for i in range(BLOCKS)]
        value = [jnp.where(odd, value[i + 1], value[i]) for i in range(BLOCKS - 1)]
        value = [jnp.where(far_pair, value[i + 2], value[i]) for i in range(rows_out + 1)]
        index, near = (lanes + turn) & (LANES - 1), lanes < LANES - turn
        value = [jnp.take_along_axis(x, index, axis=1) for x in value]
        for i in range(rows_out):
            scores[g][i] = scores[g][i] + jnp.where(near, value[i], value[i + 1])

    for part in range(2):
        for c in range(0, LN, step):
            normalise(part, c)
        for g in range(templs // 8):
            for j in range(slots // 2 * part, slots if part else slots // 2):
                align(j, g)
    for g in range(templs // 8):
        for i in range(rows_out):
            out_ref[8 * g : 8 * g + 8, LANES * i : LANES * (i + 1)] = scores[g][i]

    others = rows_of(slots_n - 1)
    pltpu.make_async_copy(others, others, send_sem).wait()


def on_device(geometry, waveforms, templates, channel_ids, moveouts, active, border, border_count):
    regions, tmpls, subs, offsets = geometry
    slots_n = tmpls * subs * len(offsets)
    chans = waveforms.shape[1]
    bmax = border.shape[2]
    templs, slots = channel_ids.shape[1:]
    wide, total = slots * templs, slots_n * chans
    by_slot = lambda x: jnp.transpose(x, (2, 0, 1))
    short_table, lag_table = wide_tables()
    gather, twiddle, steps, window = small_tables(chans)
    waves = waveforms[0].reshape(chans, RES, LANES).swapaxes(0, 1).reshape(RES * chans, LANES)
    rows = jnp.swapaxes(templates[0], 0, 1).reshape(wide, K)
    inputs = (
        waves, gather, twiddle, steps, border[0], border_count, rows, short_table,
        by_slot(channel_ids), active, by_slot(moveouts), window, lag_table,
    )
    spaces = [pltpu.VMEM] * len(inputs)
    stride = -(-(chans * SPEC_ROWS + 1) // 8) * 8
    vmem = pltpu.VMEM
    scores = pl.pallas_call(
        functools.partial(kernel, geometry, spaces, bmax),
        out_shape=pltpu.VMEM((templs, OUT), F32),
        in_specs=[pl.BlockSpec(memory_space=pltpu.HBM)] * len(inputs),
        out_specs=pl.BlockSpec(memory_space=pltpu.VMEM),
        scratch_shapes=[
            *[space(x.shape, x.dtype) for space, x in zip(spaces, inputs)],
            vmem((slots_n * stride, LANES), F32),
            vmem((wide, 2 * BAND), F32),
            vmem((wide, LANES), BF16),
            vmem((wide, LANES), jnp.int32),
            vmem((wide, 3 * total), BF16),
            vmem((wide, 3 * total), BF16),
            vmem((3 * total, 2 * BAND), BF16),
            vmem((3 * total, LN), BF16),
            vmem((total + wide, 2 * BAND), BF16),
            vmem((wide, LN), F32),
            pltpu.SemaphoreType.DMA((len(inputs),)),
            pltpu.SemaphoreType.DMA,
            pltpu.SemaphoreType.DMA((len(offsets),)),
            pltpu.SemaphoreType.REGULAR((slots_n,)),
        ],
        compiler_params=pltpu.CompilerParams(
            collective_id=0, has_side_effects=True
        ),
        name="detect",
    )(*inputs)
    return scores[None]


def solution(mesh):
    regions, tmpls, subs = (mesh.shape[a] for a in ("region", "tmpl", "sub"))
    offsets = tuple(dict.fromkeys((0, (regions - 1) % regions, 1 % regions)))
    geometry = (regions, tmpls, subs, offsets)
    in_specs = (
        P("region", ("tmpl", "sub"), "groups"),
        P("region", ("tmpl", "sub"), None, None),
        P("region", ("tmpl", "sub"), None),
        P("region", ("tmpl", "sub"), None),
        P("region", ("tmpl", "sub")),
        P("region", None, None),
        P("region", None),
    )
    return jax.shard_map(
        functools.partial(on_device, geometry),
        mesh=mesh,
        in_specs=in_specs,
        out_specs=P("region", ("tmpl", "sub"), "groups"),
        check_vma=False,
    )
```
